32 devices in a mesh: gx: 4 (over y, core), gy: 4 (over z), lev: 2 (over x).
Axes of the slice: x: 2, y: 2, z: 4, core: 2. Of those that a mesh axis runs over, the one named last changes fastest.
Arguments:
- east_wind: float32 [136, 128, 512], P('lev', 'gx', 'gy'), may hold values from -6 to 6
- north_wind: float32 [136, 128, 512], P('lev', 'gx', 'gy'), may hold values from -6 to 6
- height: float32 [136, 128, 512], P('lev', 'gx', 'gy'), may hold values from -6 to 6
- to_modes: float32 [136, 136], replicated, may hold values from -0.5 to 0.5
- to_levels: float32 [136, 136], replicated, may hold values from -0.5 to 0.5
- mode_coef: float32 [136], replicated, may hold values from 0.05 to 20
Outputs:
- east_next: float32 [136, 128, 512], P('lev', 'gx', 'gy')
- north_next: float32 [136, 128, 512], P('lev', 'gx', 'gy')
- height_next: float32 [136, 128, 512], P('lev', 'gx', 'gy')
The draws below stay inside these ranges and needn't reach their ends.
All inputs are finite; a program needn't handle non-finite values.
Results may differ from the reference program's by a relative error of at most 0.000073.
Values sent between devices are 32-bit elements; how exact they have to be, the bound alone decides.
No kernel may reach another device: no remote copies, remote signals or barrier semaphores. Data moves between devices by JAX's collectives and lax.ppermute only.
A program may use at most 64 MiB of HBM per device.

```python
import math
import jax
import jax.numpy as jnp
from jax import lax

L = 136
SWEEPS = 6
NX = 128
NY = 512


def steps_of(own_key, shape, shards, smallest, largest):
    level, own = 1.0, jax.random.fold_in(own_key, 6)
    for dim, shards_of in shards:
        steps = jnp.exp(jax.random.uniform(jax.random.fold_in(own, dim), (shards_of,), jnp.float32, smallest / len(shards), largest / len(shards)))
        level = level * jnp.repeat(steps, shape[dim] // shards_of).reshape([-1 if axis == dim else 1 for axis in range(len(shape))])
    return level


def noise(stream_key, dims, spread, limit, split=(), held_as=jnp.bfloat16):
    array = jax.random.normal(stream_key, dims, jnp.float32) * spread
    if len(split) > 0:
        array = steps_of(stream_key, dims, split, -0.22, 0.18) * array
    return jnp.clip(array, min=-limit, max=limit).astype(held_as)


def setup_inputs(seed: int = 0) -> dict:
    seeds = jax.random.split(jax.random.key(seed), 7)
    east_wind = noise(seeds[0], (L, NX, NY), 1.0, 6.0, ((0, 2), (1, 4), (2, 4)), jnp.float32)
    north_wind = noise(seeds[1], (L, NX, NY), 1.0, 6.0, ((0, 2), (1, 4), (2, 4)), jnp.float32)
    height = noise(seeds[2], (L, NX, NY), 1.0, 6.0, ((0, 2), (1, 4), (2, 4)), jnp.float32)
    to_modes = noise(seeds[3], (L, L), L ** -0.5, 0.5, (), jnp.float32)
    to_levels = noise(seeds[4], (L, L), L ** -0.5, 0.5, (), jnp.float32)
    mode_coef = jnp.clip(jnp.exp(jax.random.uniform(seeds[5], (L,), jnp.float32, math.log(0.05), math.log(20.0))), 0.05, 20.0)
    return {"east_wind": east_wind, "north_wind": north_wind, "height": height, "to_modes": to_modes, "to_levels": to_levels, "mode_coef": mode_coef}


def east_diff(padded):
    return (8.0 * (padded[..., 3:-1, 2:-2] - padded[..., 1:-3, 2:-2]) - (padded[..., 4:, 2:-2] - padded[..., :-4, 2:-2])) / 12.0


def north_diff(padded):
    return (8.0 * (padded[..., 2:-2, 3:-1] - padded[..., 2:-2, 1:-3]) - (padded[..., 2:-2, 4:] - padded[..., 2:-2, :-4])) / 12.0


def widen(field, width):
    return jnp.pad(field, ((0, 0), (width, width), (width, width)))


def project(matrix, field):
    flat = field.reshape(field.shape[0], -1)
    mixed = jnp.dot(matrix, flat, precision=lax.Precision.HIGHEST, preferred_element_type=jnp.float32)
    return mixed.reshape(field.shape)


def reference(east_wind, north_wind, height, to_modes, to_levels, mode_coef):
    diverge = east_diff(widen(east_wind, 2)) + north_diff(widen(north_wind, 2))
    source = height - diverge
    modal = project(to_modes, source)
    stiff = mode_coef[:, None, None]
    solved = modal / (1.0 + 4.0 * stiff)
    for sweep_index in range(SWEEPS):
        padded = widen(solved, 1)
        beside_all = padded[:, 2:, 1:-1] + padded[:, :-2, 1:-1] + padded[:, 1:-1, 2:] + padded[:, 1:-1, :-2]
        solved = (modal + stiff * beside_all) / (1.0 + 4.0 * stiff)
    height_next = project(to_levels, solved)
    padded = widen(height_next, 2)
    return east_wind - east_diff(padded), north_wind - north_diff(padded), height_next
```

```python
import functools

import jax
import jax.numpy as jnp
from jax import lax
from jax.experimental import pallas as pl
from jax.experimental.pallas import tpu as pltpu
from jax.sharding import PartitionSpec as P

SWEEPS = 6
HALO = SWEEPS + 2
TERMS = SWEEPS + 1
LANES = 128
VMEM = pl.BlockSpec(memory_space=pltpu.VMEM)
SMEM = pl.BlockSpec(memory_space=pltpu.SMEM)
F32 = jnp.float32
BF16 = jnp.bfloat16


def up_to(n, k):
    return (n + k - 1) // k * k


def lanes_of():
    return lax.broadcasted_iota(jnp.int32, (1, LANES), 1)


def call(body, outs, *args, specs=None, scratch=(), vmem=48 << 20, name):
    return pl.pallas_call(
        body,
        out_shape=outs,
        in_specs=specs or [VMEM] * len(args),
        out_specs=jax.tree.map(lambda _: VMEM, outs),
        scratch_shapes=list(scratch),
        compiler_params=pltpu.CompilerParams(vmem_limit_bytes=vmem),
        name=name,
    )(*args)


def row_of(ref, x):
    levels, rows, lanes = ref.shape
    return ref.reshape(levels * rows, lanes)[pl.ds(x, levels, stride=rows), :]


def set_row(ref, x, value):
    levels, rows, lanes = ref.shape
    ref.reshape(levels * rows, lanes)[pl.ds(x, levels, stride=rows), :] = value


def north_step(main, side):
    lane = lanes_of()
    one = pltpu.roll(jnp.where(lane < 1, side, main), LANES - 1, 1) - pltpu.roll(
        jnp.where(lane >= LANES - 1, side, main), 1, 1
    )
    two = pltpu.roll(jnp.where(lane < 2, side, main), LANES - 2, 1) - pltpu.roll(
        jnp.where(lane >= LANES - 2, side, main), 2, 1
    )
    return 8.0 * one - two


def wind_edges(u_ref, v_ref, lo_ref, hi_ref, cols_ref):
    levels, rows, _ = u_ref.shape
    lane = lanes_of()
    for i in range(2):
        lo_ref[i, :levels] = row_of(u_ref, i)
        hi_ref[i, :levels] = row_of(u_ref, rows - 2 + i)

    def body(x, packed):
        rolled = pltpu.roll(row_of(v_ref, x), 4 * x + 2, 1)
        return jnp.where(lane // 4 == x, rolled, packed)

    cols_ref[:levels] = lax.fori_loop(0, rows, body, jnp.zeros((levels, LANES), F32), unroll=4)


def source_rows(u_ref, v_ref, h_ref, ulo_ref, uhi_ref, vl_ref, vr_ref, edge_ref, mid_ref, lo_ref, hi_ref):
    levels, rows, _ = u_ref.shape
    lane = lanes_of()
    vside = jnp.where(lane % 4 < 2, vl_ref[:levels], vr_ref[:levels])
    pad = edge_ref.shape[1] - levels

    def at(x):
        if x < 0:
            return ulo_ref[2 + x, :levels]
        if x >= rows:
            return uhi_ref[x - rows, :levels]
        return row_of(u_ref, x)

    packs = {}
    for x in range(rows):
        v = row_of(v_ref, x)
        side = pltpu.roll(vside, (LANES - 4 * x - 2) % LANES, 1)
        dx = 8.0 * (at(x + 1) - at(x - 1)) - (at(x + 2) - at(x - 2))
        dy = north_step(v, side)
        s = row_of(h_ref, x) - (dx + dy) * (1.0 / 12.0)
        m, k = divmod(x, 8)
        if x < HALO:
            targets = [(edge_ref, x), (lo_ref, x)]
        elif x >= rows - HALO:
            targets = [(edge_ref, x - rows + 2 * HALO), (hi_ref, x - rows + HALO)]
        else:
            targets = [(mid_ref, x - HALO)]
            rolled = pltpu.roll(s, 16 * k + 8, 1)
            packs[m] = jnp.where(lane // 16 == k, rolled, packs[m]) if m in packs else rolled
            if k == 7:
                targets_pack = 2 * HALO + m - 1
                edge_ref[targets_pack, :levels] = packs[m]
                if pad:
                    edge_ref[targets_pack, levels:] = jnp.zeros((pad, LANES), F32)
        for ref, i in targets:
            ref[i, :levels] = s
            if pad:
                ref[i, levels:] = jnp.zeros((pad, LANES), F32)


def column_messages(edge_ref, below_ref, above_ref, right_ref, left_ref):
    lane = lanes_of()
    slot = lane % 16

    def pack(ref, base):
        packed = pltpu.roll(ref[base], 8, 1)
        for k in range(1, 8):
            packed = jnp.where(lane // 16 == k, pltpu.roll(ref[base + k], 16 * k + 8, 1), packed)
        return packed

    mids = edge_ref.shape[0] - 2 * HALO
    packs = [pack(below_ref, 0), pack(edge_ref, 0)]
    packs += [edge_ref[2 * HALO + i] for i in range(mids)]
    packs += [pack(edge_ref, HALO), pack(above_ref, 0)]
    for i in range(len(packs) // 2):
        even, odd = packs[2 * i], packs[2 * i + 1]
        right_ref[i] = jnp.where(slot < 8, even, pltpu.roll(odd, 8, 1))
        left_ref[i] = jnp.where(slot < 8, pltpu.roll(even, LANES - 8, 1), odd)


def weights(levels_ref, modes_ref, coef_ref, out_ref):
    levels = levels_ref.shape[0]
    lp = out_ref.shape[0] // TERMS
    kp = out_ref.shape[1] // 3
    groups = modes_ref.shape[1]
    coef = coef_ref[...]
    denom = 1.0 + 4.0 * coef
    scaled = levels_ref[...] / denom
    ratio = coef / denom
    out_ref[...] = jnp.zeros(out_ref.shape, BF16)
    for j in range(TERMS):
        m = jnp.dot(scaled, modes_ref[...], precision=lax.Precision.HIGHEST, preferred_element_type=F32)
        high = m.astype(BF16)
        low = (m - high.astype(F32)).astype(BF16)
        rows = pl.ds(j * lp, lp)
        out_ref[rows, :kp] = high
        out_ref[rows, kp : 2 * kp] = high
        out_ref[rows, 2 * kp :] = low
        scaled = scaled * ratio


def finish(place_ref, *refs, groups, limits):
    ins, refs = refs[: 7 * groups], refs[7 * groups :]
    u_ref, v_ref, east_ref, north_ref, height_ref, s_ref, t_ref, ga_ref, gb_ref = refs
    levels, rows, _ = u_ref.shape
    span = rows + 2 * HALO
    lp = ga_ref.shape[1]
    kp = s_ref.shape[2] // 3
    lane = lanes_of()
    slot = lane % 16
    sided = (lane < HALO) | (lane >= LANES - HALO)

    for g in range(groups):
        edge, mid, below, above, from_left, from_right, w = ins[7 * g : 7 * g + 7]
        for m in range(span // 8):
            zl, zr = from_left[m // 2], from_right[m // 2]
            if m % 2 == 0:
                side = jnp.where(slot < 8, zl, pltpu.roll(zr, 8, 1))
            else:
                side = jnp.where(slot < 8, pltpu.roll(zl, LANES - 8, 1), zr)
            if m == 0:
                ref, base = below, 0
            elif m == 1:
                ref, base = edge, 0
            elif m == span // 8 - 2:
                ref, base = edge, HALO
            elif m == span // 8 - 1:
                ref, base = above, 0
            else:
                ref, base = mid, 8 * (m - 2)

            for k in range(8):
                beside = jnp.where(sided, pltpu.roll(side, LANES - 16 * k - 8, 1), 0.0)
                both = jnp.concatenate([ref[base + k], beside], axis=1)
                if kp > lp:
                    both = jnp.concatenate([both, jnp.zeros((kp - lp, 2 * LANES), F32)], axis=0)
                high = both.astype(BF16)
                low = (both - high.astype(F32)).astype(BF16)
                s_ref[g, 8 * m + k, :kp] = high
                s_ref[g, 8 * m + k, kp : 2 * kp] = low
                s_ref[g, 8 * m + k, 2 * kp :] = high

    def mix(x, _):
        total = None
        for g in range(groups):
            part = jnp.dot(ins[7 * g + 6][...], s_ref[g, x], preferred_element_type=F32)
            total = part if total is None else total + part
        for j in range(TERMS):
            t_ref[j, x] = total[j * lp : (j + 1) * lp]
        return _

    lax.fori_loop(0, span, mix, 0)

    first_row = place_ref[0] * rows - HALO
    open_left = (place_ref[1] > 0) & (lane >= LANES - HALO)
    open_right = (place_ref[1] < limits[1] - 1) & (lane < HALO)
    side_mask = jnp.where(open_left | open_right, 1.0, 0.0)
    now = t_ref.at[SWEEPS]
    for step in range(SWEEPS):
        j = SWEEPS - 1 - step
        nxt = (ga_ref, gb_ref)[step % 2]

        def sweep(x, _, now=now, nxt=nxt, j=j):
            row = first_row + x
            inside = jnp.where((row >= 0) & (row < limits[0] * rows), 1.0, 0.0)
            main, side = now[x, :, :LANES], now[x, :, LANES:]
            left = pltpu.roll(jnp.where(lane == LANES - 1, side, main), 1, 1)
            right = pltpu.roll(jnp.where(lane == 0, side, main), LANES - 1, 1)
            beside = now[x - 1, :, :LANES] + now[x + 1, :, :LANES]
            nxt[x, :, :LANES] = ((beside + (left + right)) + t_ref[j, x, :, :LANES]) * inside
            left = pltpu.roll(jnp.where(lane == LANES - 1, main, side), 1, 1)
            right = pltpu.roll(jnp.where(lane == 0, main, side), LANES - 1, 1)
            beside = now[x - 1, :, LANES:] + now[x + 1, :, LANES:]
            nxt[x, :, LANES:] = ((beside + (left + right)) + t_ref[j, x, :, LANES:]) * (inside * side_mask)
            return _

        reach = j + 2
        lax.fori_loop(HALO - reach, HALO + rows + reach, sweep, 0, unroll=2)
        now = nxt

    def output(x, _):
        main, side = now[x + HALO, :levels, :LANES], now[x + HALO, :levels, LANES:]
        dy = north_step(main, side)

        def at(i):
            return now[x + HALO + i, :levels, :LANES]

        dx = 8.0 * (at(1) - at(-1)) - (at(2) - at(-2))
        set_row(east_ref, x, row_of(u_ref, x) - dx * (1.0 / 12.0))
        set_row(north_ref, x, row_of(v_ref, x) - dy * (1.0 / 12.0))
        set_row(height_ref, x, main)
        return _

    lax.fori_loop(0, rows, output, 0, unroll=2)


def shape(*dims, dtype=F32):
    return jax.ShapeDtypeStruct(dims, dtype)


def neighbours(axis):
    peers = lax.axis_size(axis)
    up = [(i, i + 1) for i in range(peers - 1)]
    return up, [(j, i) for i, j in up]


def on_device(east_wind, north_wind, height, to_modes, to_levels, mode_coef):
    levels, rows, cols = east_wind.shape
    groups = lax.axis_size("lev")
    limits = (lax.axis_size("gx"), lax.axis_size("gy"))
    lp, kp = up_to(levels, 8), up_to(levels, 16)
    span = rows + 2 * HALO
    x_up, x_down = neighbours("gx")
    y_up, y_down = neighbours("gy")

    lo, hi, packed = call(
        wind_edges,
        (shape(2, lp, LANES), shape(2, lp, LANES), shape(lp, LANES)),
        east_wind,
        north_wind,
        name="wind_edges",
    )
    u_below = lax.ppermute(hi, "gx", x_up)
    u_above = lax.ppermute(lo, "gx", x_down)
    v_left = lax.ppermute(packed, "gy", y_up)
    v_right = lax.ppermute(packed, "gy", y_down)

    mids = (rows - 2 * HALO) // 8
    edge, mid, low, high = call(
        source_rows,
        (
            shape(2 * HALO + mids, lp, LANES),
            shape(rows - 2 * HALO, lp, LANES),
            shape(HALO, lp, LANES),
            shape(HALO, lp, LANES),
        ),
        east_wind,
        north_wind,
        height,
        u_below,
        u_above,
        v_left,
        v_right,
        name="source_rows",
    )

    me = lax.axis_index("lev")
    my_levels = lax.dynamic_slice_in_dim(to_levels, me * levels, levels, 0)
    my_levels = jnp.pad(my_levels, ((0, lp - levels), (0, 0)))
    operands = []
    for d in range(groups):
        other = (me + d) % groups
        modes = lax.dynamic_slice_in_dim(to_modes, other * levels, levels, 1)
        modes = jnp.pad(modes, ((0, 0), (0, kp - levels)))
        w = call(
            weights,
            shape(TERMS * lp, 3 * kp, dtype=BF16),
            my_levels,
            modes,
            mode_coef.reshape(1, -1),
            name="weights",
        )
        if d == 0:
            e, c, l, h = edge, mid, low, high
        else:
            pairs = [((i + d) % groups, i) for i in range(groups)]
            e = lax.ppermute(edge, "lev", pairs)
            c = lax.ppermute(mid, "lev", pairs)
            l, h = e[:HALO], e[HALO : 2 * HALO]
        below = lax.ppermute(h, "gx", x_up)
        above = lax.ppermute(l, "gx", x_down)
        right, left = call(
            column_messages,
            (shape(span // 16, lp, LANES), shape(span // 16, lp, LANES)),
            e,
            below,
            above,
            name="column_messages",
        )
        from_left = lax.ppermute(right, "gy", y_up)
        from_right = lax.ppermute(left, "gy", y_down)
        operands += [e, c, below, above, from_left, from_right, w]

    place = jnp.stack([lax.axis_index("gx"), lax.axis_index("gy")]).astype(jnp.int32)
    out = shape(levels, rows, cols)
    return call(
        functools.partial(finish, groups=groups, limits=limits),
        (out, out, out),
        place,
        *operands,
        east_wind,
        north_wind,
        specs=[SMEM] + [VMEM] * (len(operands) + 2),
        scratch=(
            pltpu.VMEM((groups, span, 3 * kp, 2 * LANES), BF16),
            pltpu.VMEM((TERMS, span, lp, 2 * LANES), F32),
            pltpu.VMEM((span, lp, 2 * LANES), F32),
            pltpu.VMEM((span, lp, 2 * LANES), F32),
        ),
        vmem=60 << 20,
        name="finish",
    )


def solution(mesh):
    return jax.shard_map(
        on_device,
        mesh=mesh,
        in_specs=(P("lev", "gx", "gy"), P("lev", "gx", "gy"), P("lev", "gx", "gy"), P(), P(), P()),
        out_specs=(P("lev", "gx", "gy"), P("lev", "gx", "gy"), P("lev", "gx", "gy")),
        check_vma=False,
    )
```

```python
import functools

import jax
import jax.numpy as jnp
from jax import lax
from jax.experimental import pallas as pl
from jax.experimental.pallas import tpu as pltpu
from jax.sharding import PartitionSpec as P

SWEEPS = 6
HALO = SWEEPS + 2
TERMS = SWEEPS + 1
LANES = 128
VMEM = pl.BlockSpec(memory_space=pltpu.VMEM)
SMEM = pl.BlockSpec(memory_space=pltpu.SMEM)
ANY = pl.BlockSpec(memory_space=pl.ANY)
F32 = jnp.float32
BF16 = jnp.bfloat16


def up_to(n, k):
    return (n + k - 1) // k * k


def lanes_of():
    return lax.broadcasted_iota(jnp.int32, (1, LANES), 1)


def call(body, outs, *args, specs=None, out_specs=None, scratch=(), vmem=48 << 20, name):
    return pl.pallas_call(
        body,
        out_shape=outs,
        in_specs=specs or [VMEM] * len(args),
        out_specs=out_specs or jax.tree.map(lambda _: VMEM, outs),
        scratch_shapes=list(scratch),
        compiler_params=pltpu.CompilerParams(vmem_limit_bytes=vmem),
        name=name,
    )(*args)


def start_rows(src_ref, dst_ref, sems):
    copies = [pltpu.make_async_copy(src_ref.at[:, x, :], dst_ref.at[x], sems.at[x]) for x in range(dst_ref.shape[0])]
    for copy in copies:
        copy.start()
    return copies


def north_step(main, side):
    lane = lanes_of()
    one = pltpu.roll(jnp.where(lane < 1, side, main), LANES - 1, 1) - pltpu.roll(
        jnp.where(lane >= LANES - 1, side, main), 1, 1
    )
    two = pltpu.roll(jnp.where(lane < 2, side, main), LANES - 2, 1) - pltpu.roll(
        jnp.where(lane >= LANES - 2, side, main), 2, 1
    )
    return 8.0 * one - two


def wind_edges(u_ref, v_ref, lo_ref, hi_ref, cols_ref, v_rows, v_sems, u_sems):
    rows = u_ref.shape[1]
    lane = lanes_of()
    loads = start_rows(v_ref, v_rows, v_sems)
    edges = []
    for i in range(2):
        edges.append(pltpu.make_async_copy(u_ref.at[:, i, :], lo_ref.at[i], u_sems.at[i]))
        edges.append(pltpu.make_async_copy(u_ref.at[:, rows - 2 + i, :], hi_ref.at[i], u_sems.at[2 + i]))
    for copy in edges:
        copy.start()
    packed = None
    for x in range(rows):
        loads[x].wait()
        rolled = pltpu.roll(v_rows[x], (4 * x + 2) % LANES, 1)
        packed = rolled if packed is None else jnp.where(lane // 4 == x, rolled, packed)
    cols_ref[...] = packed
    for copy in edges:
        copy.wait()


def source_rows(
    u_ref, v_ref, h_ref, ulo_ref, uhi_ref, vl_ref, vr_ref, edge_ref, mid_ref, lo_ref, hi_ref, u_rows, v_rows, h_rows, sems
):
    rows, levels, _ = u_rows.shape
    lane = lanes_of()
    u_loads = start_rows(u_ref, u_rows, sems.at[0])
    v_loads = start_rows(v_ref, v_rows, sems.at[1])
    h_loads = start_rows(h_ref, h_rows, sems.at[2])
    vside = jnp.where(lane % 4 < 2, vl_ref[...], vr_ref[...])
    pad = edge_ref.shape[1] - levels

    def at(x):
        if x < 0:
            return ulo_ref[2 + x]
        if x >= rows:
            return uhi_ref[x - rows]
        return u_rows[x]

    def put(ref, i, value):
        ref[i, :levels] = value
        if pad:
            ref[i, levels:] = jnp.zeros((pad, LANES), F32)

    packed = None
    for x in range(rows):
        for i in range(0 if x == 0 else x + 2, min(x + 3, rows)):
            u_loads[i].wait()
        v_loads[x].wait()
        h_loads[x].wait()
        side = pltpu.roll(vside, (LANES - 4 * x - 2) % LANES, 1)
        dx = 8.0 * (at(x + 1) - at(x - 1)) - (at(x + 2) - at(x - 2))
        s = h_rows[x] - (dx + north_step(v_rows[x], side)) * (1.0 / 12.0)
        m, k = divmod(x, 8)
        if x < HALO:
            put(edge_ref, x, s)
            put(lo_ref, x, s)
        elif x >= rows - HALO:
            put(edge_ref, x - rows + 2 * HALO, s)
            put(hi_ref, x - rows + HALO, s)
        else:
            put(mid_ref, x - HALO, s)
            rolled = pltpu.roll(s, (16 * k + 8) % LANES, 1)
            packed = rolled if k == 0 else jnp.where(lane // 16 == k, rolled, packed)
            if k == 7:
                put(edge_ref, 2 * HALO + m - 1, packed)


def column_messages(edge_ref, below_ref, above_ref, right_ref, left_ref):
    lane = lanes_of()
    slot = lane % 16

    def pack(ref, base):
        packed = pltpu.roll(ref[base], 8, 1)
        for k in range(1, 8):
            packed = jnp.where(lane // 16 == k, pltpu.roll(ref[base + k], (16 * k + 8) % LANES, 1), packed)
        return packed

    mids = edge_ref.shape[0] - 2 * HALO
    packs = [pack(below_ref, 0), pack(edge_ref, 0)]
    packs += [edge_ref[2 * HALO + i] for i in range(mids)]
    packs += [pack(edge_ref, HALO), pack(above_ref, 0)]
    for i in range(len(packs) // 2):
        even, odd = packs[2 * i], packs[2 * i + 1]
        right_ref[i] = jnp.where(slot < 8, even, pltpu.roll(odd, 8, 1))
        left_ref[i] = jnp.where(slot < 8, pltpu.roll(even, LANES - 8, 1), odd)


def weights(levels_ref, modes_ref, coef_ref, out_ref):
    kp = out_ref.shape[0] // 3
    coef = coef_ref[...]
    denom = 1.0 + 4.0 * coef
    scaled = levels_ref[...] / denom
    ratio = coef / denom
    for j in range(TERMS):
        m = jnp.dot(scaled, modes_ref[...], precision=lax.Precision.HIGHEST, preferred_element_type=F32).T
        high = m.astype(BF16)
        low = (m - high.astype(F32)).astype(BF16)
        at = pl.ds(j * LANES, LANES)
        out_ref[:kp, at] = high
        out_ref[kp : 2 * kp, at] = high
        out_ref[2 * kp :, at] = low
        scaled = scaled * ratio


def level_part(place_ref, *refs, first, last, limits):
    (edge, mid, below, above, from_left, from_right, w), refs = refs[:7], refs[7:]
    if not first:
        before, refs = refs[0], refs[1:]
    if last:
        u_ref, v_ref, east_ref, north_ref, height_ref, t_ref, ga_ref, gb_ref, side_ref = refs[:9]
        u_rows, v_rows, h_rows, sems = refs[9:]
        loads = start_rows(u_ref, u_rows, sems.at[0]) + start_rows(v_ref, v_rows, sems.at[1])
    else:
        out_ref, t_ref, ga_ref, gb_ref, side_ref = refs
    span, wide, _ = ga_ref.shape
    rows = span - 2 * HALO
    lp = edge.shape[1]
    kp = w.shape[0] // 3
    slot = lanes_of() % 16

    for g_ref in (ga_ref, gb_ref):
        g_ref[:, :8] = jnp.zeros((span, 8, LANES), F32)
        g_ref[:, wide - 8 :] = jnp.zeros((span, 8, LANES), F32)

    def mixed(value):
        if kp > lp:
            value = jnp.concatenate([value, jnp.zeros((kp - lp, LANES), F32)], axis=0)
        high = value.astype(BF16)
        low = (value - high.astype(F32)).astype(BF16)
        both = jnp.concatenate([high, low, high], axis=0)
        return lax.dot_general(both, w[...], (((0,), (0,)), ((), ())), preferred_element_type=F32)

    def put(x, col, part):
        n = part.shape[0]
        for j in range(SWEEPS):
            t_ref[j, x, pl.ds(col, n)] = part[:, j * LANES : (j + 1) * LANES]
        ga_ref[x, pl.ds(col + 8, n)] = part[:, SWEEPS * LANES :]

    def rows_from(ref, at, count, x0):
        def body(i, _):
            put(x0 + i, HALO, mixed(ref[at + i]))
            return _

        lax.fori_loop(0, count, body, 0, unroll=2)

    rows_from(edge, 0, HALO, HALO)
    rows_from(mid, 0, rows - 2 * HALO, 2 * HALO)
    rows_from(edge, HALO, HALO, rows)
    rows_from(below, 0, HALO, 0)
    rows_from(above, 0, HALO, rows + HALO)
    for m in range(span // 8):
        zl, zr = from_left[m // 2], from_right[m // 2]
        if m % 2 == 0:
            side_ref[m] = jnp.where(slot < 8, zl, pltpu.roll(zr, 8, 1))
        else:
            side_ref[m] = jnp.where(slot < 8, pltpu.roll(zl, LANES - 8, 1), zr)

    def beside(m, _):
        part = mixed(side_ref[m])
        for k in range(8):
            put(8 * m + k, 0, part[16 * k : 16 * k + 8])
            put(8 * m + k, HALO + LANES, part[16 * k + 8 : 16 * k + 16])
        return _

    lax.fori_loop(0, span // 8, beside, 0)

    first_row = place_ref[0] * rows - HALO
    left = jnp.where(place_ref[1] > 0, 1.0, 0.0)
    right = jnp.where(place_ref[1] < limits[1] - 1, 1.0, 0.0)
    for step in range(SWEEPS):
        j = SWEEPS - 1 - step
        now, nxt = ((ga_ref, gb_ref), (gb_ref, ga_ref))[step % 2]
        reach = j + 2
        final = j == 0

        def sweep(x, _, now=now, nxt=nxt, j=j, final=final):
            row = first_row + x
            inside = jnp.where((row >= 0) & (row < limits[0] * rows), 1.0, 0.0)
            for y in range(8, wide - 8, 8):
                here = pl.ds(y, 8)
                total = (now[x - 1, here] + now[x + 1, here]) + (now[x, pl.ds(y - 1, 8)] + now[x, pl.ds(y + 1, 8)])
                mask = inside
                if y == 8:
                    mask = inside * left
                elif y == wide - 16:
                    mask = inside * right
                total = (total + t_ref[j, x, pl.ds(y - 8, 8)]) * mask
                if final and not first:
                    total = total + before[x - HALO + 2, pl.ds(y - 8, 8)]
                if final and not last:
                    out_ref[x - HALO + 2, pl.ds(y - 8, 8)] = total
                else:
                    nxt[x, here] = total
            return _

        lax.fori_loop(HALO - reach, HALO + rows + reach, sweep, 0, unroll=2)

    if not last:
        return
    done = (gb_ref, ga_ref)[(SWEEPS - 1) % 2]
    levels = u_rows.shape[1]

    def turn(x, _):
        h_rows[x] = done[x + HALO - 2, pl.ds(16, LANES)].T[:levels]
        return _

    lax.fori_loop(0, rows + 4, turn, 0, unroll=2)
    for copy in loads:
        copy.wait()

    def stores(x):
        return [
            pltpu.make_async_copy(src, dst.at[:, x, :], sems.at[i, x])
            for i, (src, dst) in enumerate(
                ((u_rows.at[x], east_ref), (v_rows.at[x], north_ref), (h_rows.at[x + 2], height_ref))
            )
        ]

    def output(x, _):
        def north(i):
            return done[x + HALO, pl.ds(16 + i, LANES)]

        dy = (8.0 * (north(1) - north(-1)) - (north(2) - north(-2))).T[:levels]
        dx = 8.0 * (h_rows[x + 3] - h_rows[x + 1]) - (h_rows[x + 4] - h_rows[x])
        u_rows[x] = u_rows[x] - dx * (1.0 / 12.0)
        v_rows[x] = v_rows[x] - dy * (1.0 / 12.0)
        for copy in stores(x):
            copy.start()
        return _

    lax.fori_loop(0, rows, output, 0, unroll=2)
    for x in range(rows):
        for copy in stores(x):
            copy.wait()


def shape(*dims, dtype=F32):
    return jax.ShapeDtypeStruct(dims, dtype)


def neighbours(axis):
    peers = lax.axis_size(axis)
    up = [(i, i + 1) for i in range(peers - 1)]
    return up, [(j, i) for i, j in up]


def on_device(east_wind, north_wind, height, to_modes, to_levels, mode_coef):
    levels, rows, cols = east_wind.shape
    groups = lax.axis_size("lev")
    limits = (lax.axis_size("gx"), lax.axis_size("gy"))
    lp, kp = up_to(levels, 8), up_to(levels, 16)
    span = rows + 2 * HALO
    x_up, x_down = neighbours("gx")
    y_up, y_down = neighbours("gy")

    dma = pltpu.SemaphoreType.DMA
    row_block = pltpu.VMEM((rows, levels, cols), F32)
    lo, hi, packed = call(
        wind_edges,
        (shape(2, levels, LANES), shape(2, levels, LANES), shape(levels, LANES)),
        east_wind,
        north_wind,
        specs=[ANY] * 2,
        scratch=(row_block, dma((rows,)), dma((4,))),
        name="wind_edges",
    )
    u_below = lax.ppermute(hi, "gx", x_up)
    u_above = lax.ppermute(lo, "gx", x_down)
    v_left = lax.ppermute(packed, "gy", y_up)
    v_right = lax.ppermute(packed, "gy", y_down)

    mids = (rows - 2 * HALO) // 8
    edge, mid, low, high = call(
        source_rows,
        (
            shape(2 * HALO + mids, lp, LANES),
            shape(rows - 2 * HALO, lp, LANES),
            shape(HALO, lp, LANES),
            shape(HALO, lp, LANES),
        ),
        east_wind,
        north_wind,
        height,
        u_below,
        u_above,
        v_left,
        v_right,
        specs=[ANY] * 3 + [VMEM] * 4,
        scratch=(row_block, row_block, row_block, dma((3, rows))),
        name="source_rows",
    )

    me = lax.axis_index("lev")
    my_levels = lax.dynamic_slice_in_dim(to_levels, me * levels, levels, 0)
    my_levels = jnp.pad(my_levels, ((0, LANES - levels), (0, 0)))
    place = jnp.stack([lax.axis_index("gx"), lax.axis_index("gy")]).astype(jnp.int32)
    out = shape(levels, rows, cols)
    part = None
    for d in range(groups):
        other = (me + d) % groups
        modes = lax.dynamic_slice_in_dim(to_modes, other * levels, levels, 1)
        modes = jnp.pad(modes, ((0, 0), (0, kp - levels)))
        w = call(
            weights,
            shape(3 * kp, TERMS * LANES, dtype=BF16),
            my_levels,
            modes,
            mode_coef.reshape(1, -1),
            name="weights",
        )
        if d == 0:
            e, c, l, h = edge, mid, low, high
        else:
            pairs = [((i + d) % groups, i) for i in range(groups)]
            e = lax.ppermute(edge, "lev", pairs)
            c = lax.ppermute(mid, "lev", pairs)
            l, h = e[:HALO], e[HALO : 2 * HALO]
        below = lax.ppermute(h, "gx", x_up)
        above = lax.ppermute(l, "gx", x_down)
        right, left = call(
            column_messages,
            (shape(span // 16, lp, LANES), shape(span // 16, lp, LANES)),
            e,
            below,
            above,
            name="column_messages",
        )
        from_left = lax.ppermute(right, "gy", y_up)
        from_right = lax.ppermute(left, "gy", y_down)
        last = d == groups - 1
        args = [e, c, below, above, from_left, from_right, w] + ([] if part is None else [part])
        specs = [SMEM] + [VMEM] * len(args)
        scratch = [
            pltpu.VMEM((SWEEPS, span, cols + 16, LANES), F32),
            pltpu.VMEM((span, cols + 32, LANES), F32),
            pltpu.VMEM((span, cols + 32, LANES), F32),
            pltpu.VMEM((span // 8, lp, LANES), F32),
        ]
        if last:
            args += [east_wind, north_wind]
            specs += [ANY] * 2
            scratch += [row_block, row_block, pltpu.VMEM((rows + 4, levels, cols), F32), dma((3, rows))]
        part = call(
            functools.partial(level_part, first=d == 0, last=last, limits=limits),
            (out, out, out) if last else shape(rows + 4, cols + 16, LANES),
            place,
            *args,
            specs=specs,
            out_specs=(ANY, ANY, ANY) if last else VMEM,
            scratch=scratch,
            name="level_part",
        )
    return part


def solution(mesh):
    return jax.shard_map(
        on_device,
        mesh=mesh,
        in_specs=(P("lev", "gx", "gy"), P("lev", "gx", "gy"), P("lev", "gx", "gy"), P(), P(), P()),
        out_specs=(P("lev", "gx", "gy"), P("lev", "gx", "gy"), P("lev", "gx", "gy")),
        check_vma=False,
    )
```

```python
import functools

import jax
import jax.numpy as jnp
from jax import lax
from jax.experimental import pallas as pl
from jax.experimental.pallas import tpu as pltpu
from jax.sharding import PartitionSpec as P

SWEEPS = 6
HALO = SWEEPS + 2
TERMS = SWEEPS + 1
LANES = 128
VMEM = pl.BlockSpec(memory_space=pltpu.VMEM)
SMEM = pl.BlockSpec(memory_space=pltpu.SMEM)
HBM = pl.BlockSpec(memory_space=pltpu.HBM)
F32 = jnp.float32
BF16 = jnp.bfloat16


def up_to(n, k):
    return (n + k - 1) // k * k


def lanes_of():
    return lax.broadcasted_iota(jnp.int32, (1, LANES), 1)


def call(body, outs, *args, specs=None, out_specs=None, scratch=(), vmem=48 << 20, name):
    return pl.pallas_call(
        body,
        out_shape=outs,
        in_specs=specs or [VMEM] * len(args),
        out_specs=out_specs or jax.tree.map(lambda _: VMEM, outs),
        scratch_shapes=list(scratch),
        compiler_params=pltpu.CompilerParams(vmem_limit_bytes=vmem),
        name=name,
    )(*args)


def start_rows(src_ref, dst_ref, sems, rows):
    copies = {x: pltpu.make_async_copy(src_ref.at[:, x, :], dst_ref.at[x], sems.at[x]) for x in rows}
    for copy in copies.values():
        copy.start()
    return copies


def north_step(main, side):
    lane = lanes_of()
    one = pltpu.roll(jnp.where(lane < 1, side, main), LANES - 1, 1) - pltpu.roll(
        jnp.where(lane >= LANES - 1, side, main), 1, 1
    )
    two = pltpu.roll(jnp.where(lane < 2, side, main), LANES - 2, 1) - pltpu.roll(
        jnp.where(lane >= LANES - 2, side, main), 2, 1
    )
    return 8.0 * one - two


def source_row(x, at, v, h, side):
    dx = 8.0 * (at(x + 1) - at(x - 1)) - (at(x + 2) - at(x - 2))
    return h - (dx + north_step(v, side)) * (1.0 / 12.0)


def put_padded(ref, i, value):
    levels, pad = value.shape[0], ref.shape[1] - value.shape[0]
    ref[i, :levels] = value
    if pad:
        ref[i, levels:] = jnp.zeros((pad, LANES), F32)


def inner_rows(u_ref, v_ref, h_ref, lo_ref, hi_ref, cols_ref, mid_ref, u_rows, v_rows, h_rows, sems, edge_sems):
    rows = u_ref.shape[1]
    lane = lanes_of()
    edges = []
    for i in range(2):
        edges.append(pltpu.make_async_copy(u_ref.at[:, i, :], lo_ref.at[i], edge_sems.at[i]))
        edges.append(pltpu.make_async_copy(u_ref.at[:, rows - 2 + i, :], hi_ref.at[i], edge_sems.at[2 + i]))
    for copy in edges:
        copy.start()
    v_loads = start_rows(v_ref, v_rows, sems.at[0], range(rows))
    u_loads = start_rows(u_ref, u_rows, sems.at[1], range(HALO - 2, rows - HALO + 2))
    h_loads = start_rows(h_ref, h_rows, sems.at[2], range(HALO, rows - HALO))
    for copy in v_loads.values():
        copy.wait()
    packed = None
    for x in range(rows):
        rolled = pltpu.roll(v_rows[x], (4 * x + 2) % LANES, 1)
        packed = rolled if packed is None else jnp.where(lane // 4 == x, rolled, packed)
    cols_ref[...] = packed
    for copy in (*u_loads.values(), *h_loads.values()):
        copy.wait()
    for x in range(HALO, rows - HALO):
        put_padded(mid_ref, x - HALO, source_row(x, lambda i: u_rows[i], v_rows[x], h_rows[x], v_rows[x]))
    for copy in edges:
        copy.wait()


def outer_rows(
    u_ref, v_ref, h_ref, ulo_ref, uhi_ref, vl_ref, vr_ref, low_ref, high_ref, pack_ref, u_rows, v_rows, h_rows, sems
):
    rows = u_ref.shape[1]
    lane = lanes_of()
    loads = [start_rows(ref, to, sems.at[i], range(rows)) for i, (ref, to) in enumerate(((u_ref, u_rows), (v_ref, v_rows), (h_ref, h_rows)))]
    vside = jnp.where(lane % 4 < 2, vl_ref[...], vr_ref[...])

    def at(x):
        if x < 0:
            return ulo_ref[2 + x]
        if x >= rows:
            return uhi_ref[x - rows]
        return u_rows[x]

    for some in loads:
        for copy in some.values():
            copy.wait()
    packed = None
    for x in range(rows):
        side = pltpu.roll(vside, (LANES - 4 * x - 2) % LANES, 1)
        s = source_row(x, at, v_rows[x], h_rows[x], side)
        m, k = divmod(x, 8)
        if x < HALO:
            put_padded(low_ref, x, s)
        elif x >= rows - HALO:
            put_padded(high_ref, x - rows + HALO, s)
        else:
            rolled = pltpu.roll(s, (16 * k + 8) % LANES, 1)
            packed = rolled if k == 0 else jnp.where(lane // 16 == k, rolled, packed)
            if k == 7:
                put_padded(pack_ref, m - 1, packed)


def column_messages(low_ref, high_ref, pack_ref, below_ref, above_ref, right_ref, left_ref):
    lane = lanes_of()
    slot = lane % 16

    def pack(ref):
        packed = pltpu.roll(ref[0], 8, 1)
        for k in range(1, 8):
            packed = jnp.where(lane // 16 == k, pltpu.roll(ref[k], (16 * k + 8) % LANES, 1), packed)
        return packed

    packs = [pack(below_ref), pack(low_ref)]
    packs += [pack_ref[i] for i in range(pack_ref.shape[0])]
    packs += [pack(high_ref), pack(above_ref)]
    for i in range(len(packs) // 2):
        even, odd = packs[2 * i], packs[2 * i + 1]
        right_ref[i] = jnp.where(slot < 8, even, pltpu.roll(odd, 8, 1))
        left_ref[i] = jnp.where(slot < 8, pltpu.roll(even, LANES - 8, 1), odd)


def weights(levels_ref, modes_ref, coef_ref, out_ref):
    groups, _, kp = modes_ref.shape
    coef = coef_ref[...]
    denom = 1.0 + 4.0 * coef
    scaled = levels_ref[...] / denom
    ratio = coef / denom
    for j in range(TERMS):
        at = pl.ds(j * LANES, LANES)
        for g in range(groups):
            m = jnp.dot(scaled, modes_ref[g], precision=lax.Precision.HIGHEST, preferred_element_type=F32).T
            high = m.astype(BF16)
            low = (m - high.astype(F32)).astype(BF16)
            for i, part in enumerate((high, high, low)):
                out_ref[pl.ds((3 * g + i) * kp, kp), at] = part
        scaled = scaled * ratio


PARTS = 8


def finish(place_ref, w_ref, *refs, groups, limits):
    ins, refs = refs[: PARTS * groups], refs[PARTS * groups :]
    u_ref, v_ref, east_ref, north_ref, height_ref, s_ref, z_ref, t_ref, ga_ref, gb_ref, u_rows, v_rows, h_rows, sems = refs
    span, wide, _ = ga_ref.shape
    rows = span - 2 * HALO
    blocks = span // 8
    loads = [*start_rows(u_ref, u_rows, sems.at[0], range(rows)).values()]
    loads += start_rows(v_ref, v_rows, sems.at[1], range(rows)).values()
    lane = lanes_of()
    slot = lane % 16
    outer = (lane < HALO) | (lane >= LANES - HALO)
    kp = w_ref.shape[0] // (3 * groups)

    for g_ref in (ga_ref, gb_ref):
        g_ref[:, :8] = jnp.zeros((span, 8, LANES), F32)
        g_ref[:, wide - 8 :] = jnp.zeros((span, 8, LANES), F32)

    def parts(value):
        lp = value.shape[0]
        if kp > lp:
            value = jnp.concatenate([value, jnp.zeros((kp - lp, LANES), F32)], axis=0)
        high = value.astype(BF16)
        low = (value - high.astype(F32)).astype(BF16)
        return high, low, high

    for g in range(groups):
        low, high, pack, mid, below, above, left_ref, right_ref = ins[PARTS * g : PARTS * (g + 1)]
        sources = [below, low] + [mid.at[pl.ds(8 * i, 8)] for i in range(blocks - 4)] + [high, above]
        for m in range(blocks):
            fix = pack[m - 2] if 2 <= m < blocks - 2 else None

            def stage(k, _, ref=sources[m], fix=fix, m=m, g=g):
                value = ref[k]
                if fix is not None:
                    value = jnp.where(outer, pltpu.roll(fix, LANES - 16 * k - 8, 1), value)
                at = pl.ds(pl.multiple_of(k * LANES, LANES), LANES)
                for i, part in enumerate(parts(value)):
                    s_ref[m, pl.ds((3 * g + i) * kp, kp), at] = part
                return _

            lax.fori_loop(0, 8, stage, 0, unroll=4)
            zl, zr = left_ref[m // 2], right_ref[m // 2]
            if m % 2 == 0:
                side = jnp.where(slot < 8, zl, pltpu.roll(zr, 8, 1))
            else:
                side = jnp.where(slot < 8, pltpu.roll(zl, LANES - 8, 1), zr)
            for i, part in enumerate(parts(side)):
                z_ref[pl.ds((3 * g + i) * kp, kp), m * LANES : (m + 1) * LANES] = part

    def put(x, col, part):
        n = part.shape[0]
        for j in range(SWEEPS):
            t_ref[j, x, pl.ds(col, n)] = part[:, j * LANES : (j + 1) * LANES]
        ga_ref[x, pl.ds(col + 8, n)] = part[:, SWEEPS * LANES :]

    def mix(operand):
        return lax.dot_general(operand, w_ref[...], (((0,), (0,)), ((), ())), preferred_element_type=F32)

    def block(m, _):
        part = mix(s_ref[m])
        for k in range(8):
            put(8 * m + k, HALO, part[k * LANES : (k + 1) * LANES])
        return _

    lax.fori_loop(0, blocks, block, 0)
    part = mix(z_ref[...])
    for x in range(span):
        put(x, 0, part[16 * x : 16 * x + 8])
        put(x, HALO + LANES, part[16 * x + 8 : 16 * x + 16])

    first_row = place_ref[0] * rows - HALO
    left = jnp.where(place_ref[1] > 0, 1.0, 0.0)
    right = jnp.where(place_ref[1] < limits[1] - 1, 1.0, 0.0)
    for step in range(SWEEPS):
        j = SWEEPS - 1 - step
        now, nxt = ((ga_ref, gb_ref), (gb_ref, ga_ref))[step % 2]
        reach = j + 2

        def sweep(x, _, now=now, nxt=nxt, j=j):
            row = first_row + x
            inside = jnp.where((row >= 0) & (row < limits[0] * rows), 1.0, 0.0)
            for y in range(8, wide - 8, 8):
                here = pl.ds(y, 8)
                total = (now[x - 1, here] + now[x + 1, here]) + (now[x, pl.ds(y - 1, 8)] + now[x, pl.ds(y + 1, 8)])
                mask = inside
                if y == 8:
                    mask = inside * left
                elif y == wide - 16:
                    mask = inside * right
                nxt[x, here] = (total + t_ref[j, x, pl.ds(y - 8, 8)]) * mask
            return _

        lax.fori_loop(HALO - reach, HALO + rows + reach, sweep, 0, unroll=4)

    done = (gb_ref, ga_ref)[(SWEEPS - 1) % 2]
    levels = u_rows.shape[1]

    def turn(x, _):
        h_rows[x] = done[x + HALO - 2, pl.ds(16, LANES)].T[:levels]
        return _

    lax.fori_loop(0, rows + 4, turn, 0, unroll=2)
    for copy in loads:
        copy.wait()

    def stores(x):
        return [
            pltpu.make_async_copy(src, dst.at[:, x, :], sems.at[i, x])
            for i, (src, dst) in enumerate(
                ((u_rows.at[x], east_ref), (v_rows.at[x], north_ref), (h_rows.at[x + 2], height_ref))
            )
        ]

    def output(x, _):
        def north(i):
            return done[x + HALO, pl.ds(16 + i, LANES)]

        dy = (8.0 * (north(1) - north(-1)) - (north(2) - north(-2))).T[:levels]
        dx = 8.0 * (h_rows[x + 3] - h_rows[x + 1]) - (h_rows[x + 4] - h_rows[x])
        u_rows[x] = u_rows[x] - dx * (1.0 / 12.0)
        v_rows[x] = v_rows[x] - dy * (1.0 / 12.0)
        for copy in stores(x):
            copy.start()
        return _

    lax.fori_loop(0, rows, output, 0, unroll=2)
    for x in range(rows):
        for copy in stores(x):
            copy.wait()


def shape(*dims, dtype=F32):
    return jax.ShapeDtypeStruct(dims, dtype)


def neighbours(axis):
    peers = lax.axis_size(axis)
    up = [(i, i + 1) for i in range(peers - 1)]
    return up, [(j, i) for i, j in up]


def on_device(east_wind, north_wind, height, to_modes, to_levels, mode_coef):
    levels, rows, cols = east_wind.shape
    groups = lax.axis_size("lev")
    limits = (lax.axis_size("gx"), lax.axis_size("gy"))
    lp, kp = up_to(levels, 8), up_to(levels, 16)
    span = rows + 2 * HALO
    x_up, x_down = neighbours("gx")
    y_up, y_down = neighbours("gy")
    dma = pltpu.SemaphoreType.DMA
    row_block = pltpu.VMEM((rows, levels, cols), F32)

    east_wind, north_wind, height = (
        pltpu.with_memory_space_constraint(value, pltpu.HBM) for value in (east_wind, north_wind, height)
    )

    def to_others(value):
        return [value] + [
            lax.ppermute(value, "lev", [((i + d) % groups, i) for i in range(groups)]) for d in range(1, groups)
        ]

    lo, hi, packed, mid = call(
        inner_rows,
        (
            shape(2, levels, LANES),
            shape(2, levels, LANES),
            shape(levels, LANES),
            shape(rows - 2 * HALO, lp, LANES),
        ),
        east_wind,
        north_wind,
        height,
        specs=[HBM] * 3,
        scratch=(row_block, row_block, row_block, dma((3, rows)), dma((4,))),
        name="inner_rows",
    )
    mids = to_others(mid)
    halo = (
        lax.ppermute(hi, "gx", x_up),
        lax.ppermute(lo, "gx", x_down),
        lax.ppermute(packed, "gy", y_up),
        lax.ppermute(packed, "gy", y_down),
    )

    me = lax.axis_index("lev")
    my_levels = lax.dynamic_slice_in_dim(to_levels, me * levels, levels, 0)
    my_levels = jnp.pad(my_levels, ((0, LANES - levels), (0, 0)))
    modes = []
    for d in range(groups):
        part = lax.dynamic_slice_in_dim(to_modes, (me + d) % groups * levels, levels, 1)
        modes.append(jnp.pad(part, ((0, 0), (0, kp - levels))))
    w = call(
        weights,
        shape(groups * 3 * kp, TERMS * LANES, dtype=BF16),
        my_levels,
        jnp.stack(modes),
        mode_coef.reshape(1, -1),
        name="weights",
    )
    place = jnp.stack([lax.axis_index("gx"), lax.axis_index("gy")]).astype(jnp.int32)
    halo, w, place, mids = lax.optimization_barrier((halo, w, place, mids))

    low, high, pack = call(
        outer_rows,
        (shape(HALO, lp, LANES), shape(HALO, lp, LANES), shape(rows // 8 - 2, lp, LANES)),
        east_wind,
        north_wind,
        height,
        *halo,
        specs=[HBM] * 3 + [VMEM] * 4,
        scratch=(row_block, row_block, row_block, dma((3, rows))),
        name="outer_rows",
    )
    highs, lows, packs = to_others(high), to_others(low), to_others(pack)
    below = lax.ppermute(high, "gx", x_up)
    above = lax.ppermute(low, "gx", x_down)
    right, left = call(
        column_messages,
        (shape(span // 16, lp, LANES), shape(span // 16, lp, LANES)),
        low,
        high,
        pack,
        below,
        above,
        name="column_messages",
    )
    from_left = lax.ppermute(right, "gy", y_up)
    from_right = lax.ppermute(left, "gy", y_down)
    highs, lows, packs, from_left, from_right = lax.optimization_barrier((highs, lows, packs, from_left, from_right))
    belows = [below] + [lax.ppermute(h, "gx", x_up) for h in highs[1:]]
    aboves = [above] + [lax.ppermute(l, "gx", x_down) for l in lows[1:]]
    from_left, from_right = to_others(from_left), to_others(from_right)
    operands = []
    for d in range(groups):
        operands += [lows[d], highs[d], packs[d], mids[d], belows[d], aboves[d], from_left[d], from_right[d]]
    out = shape(levels, rows, cols)
    k = groups * 3 * kp
    return call(
        functools.partial(finish, groups=groups, limits=limits),
        (out, out, out),
        place,
        w,
        *operands,
        east_wind,
        north_wind,
        specs=[SMEM] + [VMEM] * (1 + len(operands)) + [HBM] * 2,
        out_specs=(HBM, HBM, HBM),
        scratch=(
            pltpu.VMEM((span // 8, k, 8 * LANES), BF16),
            pltpu.VMEM((k, span // 8 * LANES), BF16),
            pltpu.VMEM((SWEEPS, span, cols + 16, LANES), F32),
            pltpu.VMEM((span, cols + 32, LANES), F32),
            pltpu.VMEM((span, cols + 32, LANES), F32),
            row_block,
            row_block,
            pltpu.VMEM((rows + 4, levels, cols), F32),
            dma((3, rows)),
        ),
        vmem=56 << 20,
        name="finish",
    )


def solution(mesh):
    return jax.shard_map(
        on_device,
        mesh=mesh,
        in_specs=(P("lev", "gx", "gy"), P("lev", "gx", "gy"), P("lev", "gx", "gy"), P(), P(), P()),
        out_specs=(P("lev", "gx", "gy"), P("lev", "gx", "gy"), P("lev", "gx", "gy")),
        check_vma=False,
    )
```

```python
import functools

import jax
import jax.numpy as jnp
from jax import lax
from jax.experimental import pallas as pl
from jax.experimental.pallas import tpu as pltpu
from jax.sharding import PartitionSpec as P

SWEEPS = 6
HALO = SWEEPS + 2
TERMS = SWEEPS + 1
LANES = 128
VMEM = pl.BlockSpec(memory_space=pltpu.VMEM)
SMEM = pl.BlockSpec(memory_space=pltpu.SMEM)
HBM = pl.BlockSpec(memory_space=pltpu.HBM)
F32 = jnp.float32
BF16 = jnp.bfloat16

def up_to(n, k):
    return (n + k - 1) // k * k

def lanes_of():
    return lax.broadcasted_iota(jnp.int32, (1, LANES), 1)

def call(body, outs, *args, specs=None, out_specs=None, scratch=(), alias=None, vmem=12 << 20, name):
    return pl.pallas_call(
        body,
        out_shape=outs,
        in_specs=specs or [VMEM] * len(args),
        out_specs=out_specs or jax.tree.map(lambda _: VMEM, outs),
        scratch_shapes=list(scratch),
        input_output_aliases=alias or {},
        cost_estimate=pl.CostEstimate(flops=1, transcendentals=0, bytes_accessed=1),
        compiler_params=pltpu.CompilerParams(vmem_limit_bytes=vmem),
        name=name,
    )(*args)

def start_rows(src_ref, dst_ref, sems, rows):
    copies = {x: pltpu.make_async_copy(src_ref.at[:, x, :], dst_ref.at[x], sems.at[x]) for x in rows}
    for copy in copies.values():
        copy.start()
    return copies

def north_step(main, side):
    lane = lanes_of()
    one = pltpu.roll(jnp.where(lane < 1, side, main), LANES - 1, 1) - pltpu.roll(
        jnp.where(lane >= LANES - 1, side, main), 1, 1
    )
    two = pltpu.roll(jnp.where(lane < 2, side, main), LANES - 2, 1) - pltpu.roll(
        jnp.where(lane >= LANES - 2, side, main), 2, 1
    )
    return 8.0 * one - two

def source_row(x, at, v, h, side):
    dx = 8.0 * (at(x + 1) - at(x - 1)) - (at(x + 2) - at(x - 2))
    return h - (dx + north_step(v, side)) * (1.0 / 12.0)

def put_padded(ref, i, value):
    levels, pad = value.shape[0], ref.shape[1] - value.shape[0]
    ref[i, :levels] = value
    if pad:
        ref[i, levels:] = jnp.zeros((pad, LANES), F32)

def inner_rows(u_ref, v_ref, h_ref, lo_ref, hi_ref, cols_ref, mid_ref, u_rows, v_rows, h_rows, sems, edge_sems):
    rows = u_ref.shape[1]
    lane = lanes_of()
    edges = []
    for i in range(2):
        edges.append(pltpu.make_async_copy(u_ref.at[:, i, :], lo_ref.at[i], edge_sems.at[i]))
        edges.append(pltpu.make_async_copy(u_ref.at[:, rows - 2 + i, :], hi_ref.at[i], edge_sems.at[2 + i]))
    for copy in edges:
        copy.start()
    v_loads = start_rows(v_ref, v_rows, sems.at[0], range(rows))
    u_loads = start_rows(u_ref, u_rows, sems.at[1], range(HALO - 2, rows - HALO + 2))
    h_loads = start_rows(h_ref, h_rows, sems.at[2], range(HALO, rows - HALO))
    for copy in v_loads.values():
        copy.wait()
    packed = None
    for x in range(rows):
        rolled = pltpu.roll(v_rows[x], (4 * x + 2) % LANES, 1)
        packed = rolled if packed is None else jnp.where(lane // 4 == x, rolled, packed)
    cols_ref[...] = packed
    for copy in (*u_loads.values(), *h_loads.values()):
        copy.wait()
    for x in range(HALO, rows - HALO):
        put_padded(mid_ref, x - HALO, source_row(x, lambda i: u_rows[i], v_rows[x], h_rows[x], v_rows[x]))
    for copy in edges:
        copy.wait()

def outer_rows(u_ref, v_ref, h_ref, mid_ref, low_ref, high_ref, pack_ref, u_rows, v_rows, h_rows, sems):
    rows, levels, _ = u_rows.shape
    lane = lanes_of()
    ends = [*range(HALO), *range(rows - HALO, rows)]
    wide = [*range(HALO + 2), *range(rows - HALO - 2, rows)]
    loads = [
        *start_rows(v_ref, v_rows, sems.at[1], ends).values(),
        *start_rows(u_ref, u_rows, sems.at[0], wide).values(),
        *start_rows(h_ref, h_rows, sems.at[2], ends).values(),
    ]
    for m in range(pack_ref.shape[0]):
        packed = pltpu.roll(mid_ref[8 * m], 8, 1)
        for k in range(1, 8):
            packed = jnp.where(lane // 16 == k, pltpu.roll(mid_ref[8 * m + k], (16 * k + 8) % LANES, 1), packed)
        pack_ref[m] = packed
    for copy in loads:
        copy.wait()

    def at(x):
        return u_rows[x] if 0 <= x < rows else jnp.zeros((levels, LANES), F32)

    for x in ends:
        s = source_row(x, at, v_rows[x], h_rows[x], v_rows[x])
        if x < HALO:
            put_padded(low_ref, x, s)
        else:
            put_padded(high_ref, x - rows + HALO, s)

def column_terms(own_ref, left_ref, right_ref):
    slot = lanes_of() % 4
    d = jnp.where(slot < 2, left_ref[...], right_ref[...]) - own_ref[...]
    far = jnp.where(slot < 2, pltpu.roll(d, LANES - 2, 1), -pltpu.roll(d, 2, 1))
    near = jnp.where(slot == 1, -pltpu.roll(d, LANES - 1, 1), jnp.where(slot == 2, pltpu.roll(d, 1, 1), 0.0))
    return (far + 8.0 * near) * (1.0 / 12.0)

def outer_fix(low_in, high_in, pack_in, own_ref, ulo_ref, uhi_ref, vl_ref, vr_ref, low_ref, high_ref, pack_ref, edge_ref):
    levels = own_ref.shape[0]
    lane = lanes_of()
    rows = LANES // 4
    terms = column_terms(own_ref, vl_ref, vr_ref)
    edge = (lane < 2) | (lane >= LANES - 2)
    below = {0: 8.0 * ulo_ref[1] - ulo_ref[0], 1: -ulo_ref[1]}
    above = {HALO - 1: uhi_ref[1] - 8.0 * uhi_ref[0], HALO - 2: uhi_ref[0]}
    for ref_in, ref, x0, at, more in (
        (high_in, high_ref, rows - HALO, HALO, above),
        (low_in, low_ref, 0, 0, below),
    ):
        for i in range(HALO):
            add = jnp.where(edge, pltpu.roll(terms, (LANES - 4 * (x0 + i) - 2) % LANES, 1), 0.0)
            if i in more:
                add = add + more[i] * (1.0 / 12.0)
            value = ref_in[i, :levels] + add
            put_padded(ref, i, value)
            put_padded(edge_ref, at + i, value)
    slot = lane % 16
    for m in range(pack_ref.shape[0]):
        add = jnp.zeros((levels, LANES), F32)
        for k in range(8):
            x = HALO + 8 * m + k
            here = (lane // 16 == k) & (slot >= 6) & (slot < 10)
            add = jnp.where(here, pltpu.roll(terms, (16 * k + 6 - 4 * x) % LANES, 1), add)
        value = pack_in[m, :levels] + add
        put_padded(pack_ref, m, value)
        put_padded(edge_ref, 2 * HALO + m, value)


def column_messages(low_ref, high_ref, pack_ref, below_ref, above_ref, right_ref, left_ref):
    lane = lanes_of()
    slot = lane % 16

    def pack(ref):
        packed = pltpu.roll(ref[0], 8, 1)
        for k in range(1, 8):
            packed = jnp.where(lane // 16 == k, pltpu.roll(ref[k], (16 * k + 8) % LANES, 1), packed)
        return packed

    packs = [pack(below_ref), pack(low_ref)]
    packs += [pack_ref[i] for i in range(pack_ref.shape[0])]
    packs += [pack(high_ref), pack(above_ref)]
    for i in range(len(packs) // 2):
        even, odd = packs[2 * i], packs[2 * i + 1]
        right_ref[i] = jnp.where(slot < 8, even, pltpu.roll(odd, 8, 1))
        left_ref[i] = jnp.where(slot < 8, pltpu.roll(even, LANES - 8, 1), odd)

def weights(levels_ref, modes_ref, coef_ref, out_ref):
    groups, _, kp = modes_ref.shape
    coef = coef_ref[...]
    denom = 1.0 + 4.0 * coef
    scaled = levels_ref[...] / denom
    ratio = coef / denom
    for j in range(TERMS):
        at = pl.ds(j * LANES, LANES)
        for g in range(groups):
            m = jnp.dot(scaled, modes_ref[g], precision=lax.Precision.HIGHEST, preferred_element_type=F32).T
            high = m.astype(BF16)
            low = (m - high.astype(F32)).astype(BF16)
            for i, part in enumerate((high, high, low)):
                out_ref[pl.ds((3 * g + i) * kp, kp), at] = part
        scaled = scaled * ratio

def parts(value, kp):
    if kp > value.shape[0]:
        value = jnp.concatenate([value, jnp.zeros((kp - value.shape[0], LANES), F32)], axis=0)
    high = value.astype(BF16)
    low = (value - high.astype(F32)).astype(BF16)
    return high, low, high

def stage_block(s_ref, m, g, kp, ref, fix=None):
    lane = lanes_of()
    outer = (lane < HALO) | (lane >= LANES - HALO)

    def stage(k, _):
        value = ref[k]
        if fix is not None:
            value = jnp.where(outer, pltpu.roll(fix, LANES - 16 * k - 8, 1), value)
        at = pl.ds(pl.multiple_of(k * LANES, LANES), LANES)
        for i, part in enumerate(parts(value, kp)):
            s_ref[m, pl.ds((3 * g + i) * kp, kp), at] = part
        return _

    lax.fori_loop(0, 8, stage, 0, unroll=4)

def stage_sides(z_ref, g, kp, left_ref, right_ref):
    slot = lanes_of() % 16
    for m in range(z_ref.shape[1] // LANES):
        zl, zr = left_ref[m // 2], right_ref[m // 2]
        if m % 2 == 0:
            side = jnp.where(slot < 8, zl, pltpu.roll(zr, 8, 1))
        else:
            side = jnp.where(slot < 8, pltpu.roll(zl, LANES - 8, 1), zr)
        for i, part in enumerate(parts(side, kp)):
            z_ref[pl.ds((3 * g + i) * kp, kp), m * LANES : (m + 1) * LANES] = part

def mix(operand, w_ref):
    return lax.dot_general(operand, w_ref[...], (((0,), (0,)), ((), ())), preferred_element_type=F32)

def put(t_ref, g_ref, x, col, part, add):
    at = pl.ds(col, part.shape[0])
    for j in range(TERMS):
        value = part[:, j * LANES : (j + 1) * LANES]
        if j == SWEEPS:
            at = pl.ds(col + 8, part.shape[0])
            g_ref[x, at] = g_ref[x, at] + value if add else value
        else:
            t_ref[j, x, at] = t_ref[j, x, at] + value if add else value

def put_blocks(t_ref, g_ref, s_ref, w_ref, row_of_block, add):
    def block(m, _):
        part = mix(s_ref[m], w_ref)
        for k in range(8):
            put(t_ref, g_ref, row_of_block(m) + k, HALO, part[k * LANES : (k + 1) * LANES], add)
        return _

    lax.fori_loop(0, s_ref.shape[0], block, 0)

def put_sides(t_ref, g_ref, z_ref, w_ref, add):
    part = mix(z_ref[...], w_ref)
    for x in range(g_ref.shape[0]):
        put(t_ref, g_ref, x, 0, part[16 * x : 16 * x + 8], add)
        put(t_ref, g_ref, x, HALO + LANES, part[16 * x + 8 : 16 * x + 16], add)


def mix_inner(w_ref, *refs, groups):
    ins, (below, above, zl, zr, t_ref, g_ref, s_ref, r_ref, z_ref) = refs[: 2 * groups], refs[2 * groups :]
    span, wide, _ = g_ref.shape
    kp = r_ref.shape[1] // 3
    w_own = w_ref.at[pl.ds(0, 3 * kp)]
    g_ref[:, :8] = jnp.zeros((span, 8, LANES), F32)
    g_ref[:, wide - 8 :] = jnp.zeros((span, 8, LANES), F32)
    stage_block(r_ref, 0, 0, kp, below)
    stage_block(r_ref, 1, 0, kp, above)
    stage_sides(z_ref, 0, kp, zl, zr)
    put_blocks(t_ref, g_ref, r_ref, w_own, lambda m: m * (span - HALO), False)
    put_sides(t_ref, g_ref, z_ref, w_own, False)
    for g in range(groups):
        edge, mid = ins[2 * g : 2 * g + 2]
        inner = mid.shape[0] // 8
        stage_block(s_ref, 0, g, kp, edge.at[pl.ds(0, HALO)])
        for i in range(inner):
            stage_block(s_ref, 1 + i, g, kp, mid.at[pl.ds(8 * i, 8)], edge[2 * HALO + i])
        stage_block(s_ref, 1 + inner, g, kp, edge.at[pl.ds(HALO, HALO)])
    put_blocks(t_ref, g_ref, s_ref, w_ref, lambda m: HALO + 8 * m, False)


def finish(place_ref, w_ref, *refs, others, limits):
    ins, refs = refs[: 4 * others], refs[4 * others :]
    _, _, u_ref, v_ref, t_ref, ga_ref, east_ref, north_ref, height_ref, s_ref, z_ref, gb_ref, u_rows, v_rows, h_rows, sems = refs
    span, wide, _ = ga_ref.shape
    rows = span - 2 * HALO
    loads = [*start_rows(u_ref, u_rows, sems.at[0], range(rows)).values()]
    loads += start_rows(v_ref, v_rows, sems.at[1], range(rows)).values()
    gb_ref[:, :8] = jnp.zeros((span, 8, LANES), F32)
    gb_ref[:, wide - 8 :] = jnp.zeros((span, 8, LANES), F32)
    k = s_ref.shape[1]
    for d in range(others):
        below, above, zl, zr = ins[4 * d : 4 * d + 4]
        kp = k // (3 * others)
        stage_block(s_ref, 0, d, kp, below)
        stage_block(s_ref, 1, d, kp, above)
        stage_sides(z_ref, d, kp, zl, zr)
    w_others = w_ref.at[pl.ds(w_ref.shape[0] - k, k)]
    put_blocks(t_ref, ga_ref, s_ref, w_others, lambda m: m * (span - HALO), True)
    put_sides(t_ref, ga_ref, z_ref, w_others, True)

    first_row = place_ref[0] * rows - HALO
    left = jnp.where(place_ref[1] > 0, 1.0, 0.0)
    right = jnp.where(place_ref[1] < limits[1] - 1, 1.0, 0.0)
    for step in range(SWEEPS):
        j = SWEEPS - 1 - step
        now, nxt = ((ga_ref, gb_ref), (gb_ref, ga_ref))[step % 2]
        reach = j + 2

        def sweep(x, _, now=now, nxt=nxt, j=j):
            row = first_row + x
            inside = jnp.where((row >= 0) & (row < limits[0] * rows), 1.0, 0.0)
            for y in range(8, wide - 8, 8):
                here = pl.ds(y, 8)
                total = (now[x - 1, here] + now[x + 1, here]) + (now[x, pl.ds(y - 1, 8)] + now[x, pl.ds(y + 1, 8)])
                mask = inside
                if y == 8:
                    mask = inside * left
                elif y == wide - 16:
                    mask = inside * right
                nxt[x, here] = (total + t_ref[j, x, pl.ds(y - 8, 8)]) * mask
            return _

        lax.fori_loop(HALO - reach, HALO + rows + reach, sweep, 0, unroll=4)

    done = (gb_ref, ga_ref)[(SWEEPS - 1) % 2]
    levels = u_rows.shape[1]

    def turn(x, _):
        h_rows[x] = done[x + HALO - 2, pl.ds(16, LANES)].T[:levels]
        return _

    lax.fori_loop(0, rows + 4, turn, 0, unroll=2)
    for copy in loads:
        copy.wait()

    def stores(x):
        return [
            pltpu.make_async_copy(src, dst.at[:, x, :], sems.at[i, x])
            for i, (src, dst) in enumerate(
                ((u_rows.at[x], east_ref), (v_rows.at[x], north_ref), (h_rows.at[x + 2], height_ref))
            )
        ]

    def output(x, _):
        def north(i):
            return done[x + HALO, pl.ds(16 + i, LANES)]

        dy = (8.0 * (north(1) - north(-1)) - (north(2) - north(-2))).T[:levels]
        dx = 8.0 * (h_rows[x + 3] - h_rows[x + 1]) - (h_rows[x + 4] - h_rows[x])
        u_rows[x] = u_rows[x] - dx * (1.0 / 12.0)
        v_rows[x] = v_rows[x] - dy * (1.0 / 12.0)
        for copy in stores(x):
            copy.start()
        return _

    lax.fori_loop(0, rows, output, 0, unroll=2)
    for x in range(rows):
        for copy in stores(x):
            copy.wait()

def shape(*dims, dtype=F32):
    return jax.ShapeDtypeStruct(dims, dtype)

def neighbours(axis):
    peers = lax.axis_size(axis)
    up = [(i, i + 1) for i in range(peers - 1)]
    return up, [(j, i) for i, j in up]

def on_device(east_wind, north_wind, height, to_modes, to_levels, mode_coef):
    levels, rows, cols = east_wind.shape
    groups = lax.axis_size("lev")
    limits = (lax.axis_size("gx"), lax.axis_size("gy"))
    lp, kp = up_to(levels, 8), up_to(levels, 16)
    span = rows + 2 * HALO
    x_up, x_down = neighbours("gx")
    y_up, y_down = neighbours("gy")
    dma = pltpu.SemaphoreType.DMA
    row_block = pltpu.VMEM((rows, levels, cols), F32)

    east_wind, north_wind, height = (
        pltpu.with_memory_space_constraint(value, pltpu.HBM) for value in (east_wind, north_wind, height)
    )

    def to_others(value):
        return [value] + [
            lax.ppermute(value, "lev", [((i + d) % groups, i) for i in range(groups)]) for d in range(1, groups)
        ]

    lo, hi, packed, mid = call(
        inner_rows,
        (
            shape(2, levels, LANES),
            shape(2, levels, LANES),
            shape(levels, LANES),
            shape(rows - 2 * HALO, lp, LANES),
        ),
        east_wind,
        north_wind,
        height,
        specs=[HBM] * 3,
        scratch=(row_block, row_block, row_block, dma((3, rows)), dma((4,))),
        name="inner_rows",
    )
    mids = to_others(mid)
    halo = (
        lax.ppermute(hi, "gx", x_up),
        lax.ppermute(lo, "gx", x_down),
        lax.ppermute(packed, "gy", y_up),
        lax.ppermute(packed, "gy", y_down),
    )

    me = lax.axis_index("lev")
    my_levels = lax.dynamic_slice_in_dim(to_levels, me * levels, levels, 0)
    my_levels = jnp.pad(my_levels, ((0, LANES - levels), (0, 0)))
    modes = []
    for d in range(groups):
        part = lax.dynamic_slice_in_dim(to_modes, (me + d) % groups * levels, levels, 1)
        modes.append(jnp.pad(part, ((0, 0), (0, kp - levels))))
    w = call(
        weights,
        shape(groups * 3 * kp, TERMS * LANES, dtype=BF16),
        my_levels,
        jnp.stack(modes),
        mode_coef.reshape(1, -1),
        name="weights",
    )
    place = jnp.stack([lax.axis_index("gx"), lax.axis_index("gy")]).astype(jnp.int32)
    low, high, pack = call(
        outer_rows,
        (shape(HALO, lp, LANES), shape(HALO, lp, LANES), shape(rows // 8 - 2, lp, LANES)),
        east_wind,
        north_wind,
        height,
        mid,
        specs=[HBM] * 3 + [VMEM],
        scratch=(row_block, row_block, row_block, dma((3, rows))),
        name="outer_rows",
    )
    halo, w, place, mids, low, high, pack = lax.optimization_barrier((halo, w, place, mids, low, high, pack))

    mids_rows = rows // 8 - 2
    low, high, pack, edge = call(
        outer_fix,
        (
            shape(HALO, lp, LANES),
            shape(HALO, lp, LANES),
            shape(mids_rows, lp, LANES),
            shape(2 * HALO + mids_rows, lp, LANES),
        ),
        low,
        high,
        pack,
        packed,
        *halo,
        name="outer_fix",
    )
    edges = to_others(edge)
    below = lax.ppermute(high, "gx", x_up)
    above = lax.ppermute(low, "gx", x_down)
    right, left = call(
        column_messages,
        (shape(span // 16, lp, LANES), shape(span // 16, lp, LANES)),
        low,
        high,
        pack,
        below,
        above,
        name="column_messages",
    )
    from_left = lax.ppermute(right, "gy", y_up)
    from_right = lax.ppermute(left, "gy", y_down)
    edges, zl, zr = lax.optimization_barrier((edges, from_left, from_right))
    belows = [lax.ppermute(e[HALO : 2 * HALO], "gx", x_up) for e in edges[1:]]
    aboves = [lax.ppermute(e[:HALO], "gx", x_down) for e in edges[1:]]
    lefts, rights = to_others(zl), to_others(zr)

    k = 3 * kp
    operands = []
    for d in range(groups):
        operands += [edges[d], mids[d]]
    t, g = call(
        functools.partial(mix_inner, groups=groups),
        (shape(SWEEPS, span, cols + 16, LANES), shape(span, cols + 32, LANES)),
        w,
        *operands,
        below,
        above,
        zl,
        zr,
        scratch=(
            pltpu.VMEM((rows // 8, groups * k, 8 * LANES), BF16),
            pltpu.VMEM((2, k, 8 * LANES), BF16),
            pltpu.VMEM((k, span // 8 * LANES), BF16),
        ),
        name="mix_inner",
    )
    operands = []
    for d in range(groups - 1):
        operands += [belows[d], aboves[d], lefts[d + 1], rights[d + 1]]
    out = shape(levels, rows, cols)
    return call(
        functools.partial(finish, others=groups - 1, limits=limits),
        (shape(SWEEPS, span, cols + 16, LANES), shape(span, cols + 32, LANES), out, out, out),
        place,
        w,
        *operands,
        t,
        g,
        east_wind,
        north_wind,
        specs=[SMEM] + [VMEM] * (len(operands) + 3) + [HBM] * 2,
        out_specs=(VMEM, VMEM, HBM, HBM, HBM),
        scratch=(
            pltpu.VMEM((2, (groups - 1) * k, 8 * LANES), BF16),
            pltpu.VMEM(((groups - 1) * k, span // 8 * LANES), BF16),
            pltpu.VMEM((span, cols + 32, LANES), F32),
            row_block,
            row_block,
            pltpu.VMEM((rows + 4, levels, cols), F32),
            dma((3, rows)),
        ),
        alias={2 + len(operands): 0, 3 + len(operands): 1},
        name="finish",
    )[2:]


def solution(mesh):
    return jax.shard_map(
        on_device,
        mesh=mesh,
        in_specs=(P("lev", "gx", "gy"), P("lev", "gx", "gy"), P("lev", "gx", "gy"), P(), P(), P()),
        out_specs=(P("lev", "gx", "gy"), P("lev", "gx", "gy"), P("lev", "gx", "gy")),
        check_vma=False,
    )
```

```python
import functools

import jax
import jax.numpy as jnp
from jax import lax
from jax.experimental import pallas as pl
from jax.experimental.pallas import tpu as pltpu
from jax.sharding import PartitionSpec as P

SWEEPS = 6
HALO = SWEEPS + 2
TERMS = SWEEPS + 1
LANES = 128
VMEM = pl.BlockSpec(memory_space=pltpu.VMEM)
SMEM = pl.BlockSpec(memory_space=pltpu.SMEM)
HBM = pl.BlockSpec(memory_space=pltpu.HBM)
F32 = jnp.float32
BF16 = jnp.bfloat16

def up_to(n, k):
    return (n + k - 1) // k * k

def lanes_of():
    return lax.broadcasted_iota(jnp.int32, (1, LANES), 1)

def call(body, outs, *args, specs=None, out_specs=None, scratch=(), alias=None, vmem=12 << 20, name):
    return pl.pallas_call(
        body,
        out_shape=outs,
        in_specs=specs or [VMEM] * len(args),
        out_specs=out_specs or jax.tree.map(lambda _: VMEM, outs),
        scratch_shapes=list(scratch),
        input_output_aliases=alias or {},
        cost_estimate=pl.CostEstimate(flops=1, transcendentals=0, bytes_accessed=1),
        compiler_params=pltpu.CompilerParams(vmem_limit_bytes=vmem),
        name=name,
    )(*args)

def start_rows(src_ref, dst_ref, sems, rows):
    copies = {x: pltpu.make_async_copy(src_ref.at[:, x, :], dst_ref.at[x], sems.at[x]) for x in rows}
    for copy in copies.values():
        copy.start()
    return copies

def north_step(main, side):
    lane = lanes_of()
    one = pltpu.roll(jnp.where(lane < 1, side, main), LANES - 1, 1) - pltpu.roll(
        jnp.where(lane >= LANES - 1, side, main), 1, 1
    )
    two = pltpu.roll(jnp.where(lane < 2, side, main), LANES - 2, 1) - pltpu.roll(
        jnp.where(lane >= LANES - 2, side, main), 2, 1
    )
    return 8.0 * one - two

def source_row(x, at, v, h, side):
    dx = 8.0 * (at(x + 1) - at(x - 1)) - (at(x + 2) - at(x - 2))
    return h - (dx + north_step(v, side)) * (1.0 / 12.0)

def put_padded(ref, i, value):
    levels, pad = value.shape[0], ref.shape[1] - value.shape[0]
    ref[i, :levels] = value
    if pad:
        ref[i, levels:] = jnp.zeros((pad, LANES), F32)

def inner_rows(u_ref, v_ref, h_ref, lo_ref, hi_ref, cols_ref, mid_ref, u_rows, v_rows, h_rows, sems, edge_sems):
    rows = u_ref.shape[1]
    lane = lanes_of()
    edges = []
    for i in range(2):
        edges.append(pltpu.make_async_copy(u_ref.at[:, i, :], lo_ref.at[i], edge_sems.at[i]))
        edges.append(pltpu.make_async_copy(u_ref.at[:, rows - 2 + i, :], hi_ref.at[i], edge_sems.at[2 + i]))
    for copy in edges:
        copy.start()
    v_loads = start_rows(v_ref, v_rows, sems.at[0], range(rows))
    u_loads = start_rows(u_ref, u_rows, sems.at[1], range(HALO - 2, rows - HALO + 2))
    h_loads = start_rows(h_ref, h_rows, sems.at[2], range(HALO, rows - HALO))
    for copy in v_loads.values():
        copy.wait()
    packed = None
    for x in range(rows):
        rolled = pltpu.roll(v_rows[x], (4 * x + 2) % LANES, 1)
        packed = rolled if packed is None else jnp.where(lane // 4 == x, rolled, packed)
    cols_ref[...] = packed
    for copy in (*u_loads.values(), *h_loads.values()):
        copy.wait()
    for x in range(HALO, rows - HALO):
        put_padded(mid_ref, x - HALO, source_row(x, lambda i: u_rows[i], v_rows[x], h_rows[x], v_rows[x]))
    for copy in edges:
        copy.wait()

def outer_rows(u_ref, v_ref, h_ref, mid_ref, low_ref, high_ref, pack_ref, u_rows, v_rows, h_rows, sems):
    rows, levels, _ = u_rows.shape
    lane = lanes_of()
    ends = [*range(HALO), *range(rows - HALO, rows)]
    wide = [*range(HALO + 2), *range(rows - HALO - 2, rows)]
    loads = [
        *start_rows(v_ref, v_rows, sems.at[1], ends).values(),
        *start_rows(u_ref, u_rows, sems.at[0], wide).values(),
        *start_rows(h_ref, h_rows, sems.at[2], ends).values(),
    ]
    for m in range(pack_ref.shape[0]):
        packed = pltpu.roll(mid_ref[8 * m], 8, 1)
        for k in range(1, 8):
            packed = jnp.where(lane // 16 == k, pltpu.roll(mid_ref[8 * m + k], (16 * k + 8) % LANES, 1), packed)
        pack_ref[m] = packed
    for copy in loads:
        copy.wait()

    def at(x):
        return u_rows[x] if 0 <= x < rows else jnp.zeros((levels, LANES), F32)

    for x in ends:
        s = source_row(x, at, v_rows[x], h_rows[x], v_rows[x])
        if x < HALO:
            put_padded(low_ref, x, s)
        else:
            put_padded(high_ref, x - rows + HALO, s)

def column_terms(own_ref, left_ref, right_ref):
    slot = lanes_of() % 4
    d = jnp.where(slot < 2, left_ref[...], right_ref[...]) - own_ref[...]
    far = jnp.where(slot < 2, pltpu.roll(d, LANES - 2, 1), -pltpu.roll(d, 2, 1))
    near = jnp.where(slot == 1, -pltpu.roll(d, LANES - 1, 1), jnp.where(slot == 2, pltpu.roll(d, 1, 1), 0.0))
    return (far + 8.0 * near) * (1.0 / 12.0)

def outer_fix(low_in, high_in, pack_in, own_ref, ulo_ref, uhi_ref, vl_ref, vr_ref, low_ref, high_ref, pack_ref, edge_ref):
    levels = own_ref.shape[0]
    lane = lanes_of()
    rows = LANES // 4
    terms = column_terms(own_ref, vl_ref, vr_ref)
    edge = (lane < 2) | (lane >= LANES - 2)
    below = {0: 8.0 * ulo_ref[1] - ulo_ref[0], 1: -ulo_ref[1]}
    above = {HALO - 1: uhi_ref[1] - 8.0 * uhi_ref[0], HALO - 2: uhi_ref[0]}
    for ref_in, ref, x0, at, more in (
        (high_in, high_ref, rows - HALO, HALO, above),
        (low_in, low_ref, 0, 0, below),
    ):
        for i in range(HALO):
            add = jnp.where(edge, pltpu.roll(terms, (LANES - 4 * (x0 + i) - 2) % LANES, 1), 0.0)
            if i in more:
                add = add + more[i] * (1.0 / 12.0)
            value = ref_in[i, :levels] + add
            put_padded(ref, i, value)
            put_padded(edge_ref, at + i, value)
    slot = lane % 16
    for m in range(pack_ref.shape[0]):
        add = jnp.zeros((levels, LANES), F32)
        for k in range(8):
            x = HALO + 8 * m + k
            here = (lane // 16 == k) & (slot >= 6) & (slot < 10)
            add = jnp.where(here, pltpu.roll(terms, (16 * k + 6 - 4 * x) % LANES, 1), add)
        value = pack_in[m, :levels] + add
        put_padded(pack_ref, m, value)
        put_padded(edge_ref, 2 * HALO + m, value)


def column_messages(low_ref, high_ref, pack_ref, below_ref, above_ref, right_ref, left_ref):
    lane = lanes_of()
    slot = lane % 16

    def pack(ref):
        packed = pltpu.roll(ref[0], 8, 1)
        for k in range(1, 8):
            packed = jnp.where(lane // 16 == k, pltpu.roll(ref[k], (16 * k + 8) % LANES, 1), packed)
        return packed

    packs = [pack(below_ref), pack(low_ref)]
    packs += [pack_ref[i] for i in range(pack_ref.shape[0])]
    packs += [pack(high_ref), pack(above_ref)]
    for i in range(len(packs) // 2):
        even, odd = packs[2 * i], packs[2 * i + 1]
        right_ref[i] = jnp.where(slot < 8, even, pltpu.roll(odd, 8, 1))
        left_ref[i] = jnp.where(slot < 8, pltpu.roll(even, LANES - 8, 1), odd)

def weights(levels_ref, modes_ref, coef_ref, out_ref):
    groups, _, kp = modes_ref.shape
    coef = coef_ref[...]
    denom = 1.0 + 4.0 * coef
    scaled = levels_ref[...] / denom
    ratio = coef / denom
    for j in range(TERMS):
        at = pl.ds(j * LANES, LANES)
        for g in range(groups):
            m = jnp.dot(scaled, modes_ref[g], precision=lax.Precision.HIGHEST, preferred_element_type=F32).T
            high = m.astype(BF16)
            low = (m - high.astype(F32)).astype(BF16)
            for i, part in enumerate((high, high, low)):
                out_ref[pl.ds((3 * g + i) * kp, kp), at] = part
        scaled = scaled * ratio

def parts(value, kp):
    if kp > value.shape[0]:
        value = jnp.concatenate([value, jnp.zeros((kp - value.shape[0], LANES), F32)], axis=0)
    high = value.astype(BF16)
    low = (value - high.astype(F32)).astype(BF16)
    return high, low, high

def stage_block(s_ref, m, g, kp, ref, fix=None):
    lane = lanes_of()
    outer = (lane < HALO) | (lane >= LANES - HALO)

    def stage(k, _):
        value = ref[k]
        if fix is not None:
            value = jnp.where(outer, pltpu.roll(fix, LANES - 16 * k - 8, 1), value)
        at = pl.ds(pl.multiple_of(k * LANES, LANES), LANES)
        for i, part in enumerate(parts(value, kp)):
            s_ref[m, pl.ds((3 * g + i) * kp, kp), at] = part
        return _

    lax.fori_loop(0, 8, stage, 0, unroll=4)

def stage_sides(z_ref, g, kp, left_ref, right_ref):
    slot = lanes_of() % 16
    for m in range(z_ref.shape[1] // LANES):
        zl, zr = left_ref[m // 2], right_ref[m // 2]
        if m % 2 == 0:
            side = jnp.where(slot < 8, zl, pltpu.roll(zr, 8, 1))
        else:
            side = jnp.where(slot < 8, pltpu.roll(zl, LANES - 8, 1), zr)
        for i, part in enumerate(parts(side, kp)):
            z_ref[pl.ds((3 * g + i) * kp, kp), m * LANES : (m + 1) * LANES] = part

def mix(operand, w_ref):
    return lax.dot_general(operand, w_ref[...], (((0,), (0,)), ((), ())), preferred_element_type=F32)

def put(t_ref, g_ref, x, col, part, add):
    at = pl.ds(col, part.shape[0])
    for j in range(TERMS):
        value = part[:, j * LANES : (j + 1) * LANES]
        if j == SWEEPS:
            at = pl.ds(col + 8, part.shape[0])
            g_ref[x, at] = g_ref[x, at] + value if add else value
        else:
            t_ref[j, x, at] = t_ref[j, x, at] + value if add else value

def put_blocks(t_ref, g_ref, s_ref, w_ref, row_of_block, add):
    def block(m, _):
        part = mix(s_ref[m], w_ref)
        for k in range(8):
            put(t_ref, g_ref, row_of_block(m) + k, HALO, part[k * LANES : (k + 1) * LANES], add)
        return _

    lax.fori_loop(0, s_ref.shape[0], block, 0)

def put_sides(t_ref, g_ref, z_ref, w_ref, add):
    part = mix(z_ref[...], w_ref)
    for x in range(g_ref.shape[0]):
        put(t_ref, g_ref, x, 0, part[16 * x : 16 * x + 8], add)
        put(t_ref, g_ref, x, HALO + LANES, part[16 * x + 8 : 16 * x + 16], add)


def mix_outer(w_ref, low, high, below, above, t_ref, g_ref, s_ref):
    span, wide, _ = g_ref.shape
    kp = s_ref.shape[1] // 3
    g_ref[:, :8] = jnp.zeros((span, 8, LANES), F32)
    g_ref[:, wide - 8 :] = jnp.zeros((span, 8, LANES), F32)
    for m, ref in enumerate((below, low, high, above)):
        stage_block(s_ref, m, 0, kp, ref)
    far = span - 4 * HALO
    put_blocks(t_ref, g_ref, s_ref, w_ref.at[pl.ds(0, 3 * kp)], lambda m: HALO * m + jnp.where(m > 1, far, 0), False)


def mix_inner(w_ref, *refs, groups):
    ins, (zl, zr, _, _, t_ref, g_ref, s_ref, r_ref, z_ref) = refs[: 2 * groups], refs[2 * groups :]
    span, wide, _ = g_ref.shape
    k = z_ref.shape[0]
    kp = k // 3
    w_own = w_ref.at[pl.ds(0, k)]
    w_others = w_ref.at[pl.ds(k, k * (groups - 1))]
    stage_sides(z_ref, 0, kp, zl, zr)
    put_sides(t_ref, g_ref, z_ref, w_own, False)
    for g in range(groups):
        edge, mid = ins[2 * g : 2 * g + 2]
        for i in range(mid.shape[0] // 8):
            stage_block(s_ref, i, g, kp, mid.at[pl.ds(8 * i, 8)], edge[2 * HALO + i])
        if g > 0:
            stage_block(r_ref, 0, g - 1, kp, edge.at[pl.ds(0, HALO)])
            stage_block(r_ref, 1, g - 1, kp, edge.at[pl.ds(HALO, HALO)])
    put_blocks(t_ref, g_ref, r_ref, w_others, lambda m: HALO + (span - 3 * HALO) * m, True)
    put_blocks(t_ref, g_ref, s_ref, w_ref, lambda m: 2 * HALO + 8 * m, False)


def finish(place_ref, w_ref, *refs, others, limits):
    ins, refs = refs[: 4 * others], refs[4 * others :]
    _, _, u_ref, v_ref, t_ref, ga_ref, east_ref, north_ref, height_ref, s_ref, z_ref, gb_ref, u_rows, v_rows, h_rows, sems = refs
    span, wide, _ = ga_ref.shape
    rows = span - 2 * HALO
    loads = [*start_rows(u_ref, u_rows, sems.at[0], range(rows)).values()]
    loads += start_rows(v_ref, v_rows, sems.at[1], range(rows)).values()
    gb_ref[:, :8] = jnp.zeros((span, 8, LANES), F32)
    gb_ref[:, wide - 8 :] = jnp.zeros((span, 8, LANES), F32)
    k = s_ref.shape[1]
    for d in range(others):
        below, above, zl, zr = ins[4 * d : 4 * d + 4]
        kp = k // (3 * others)
        stage_block(s_ref, 0, d, kp, below)
        stage_block(s_ref, 1, d, kp, above)
        stage_sides(z_ref, d, kp, zl, zr)
    w_others = w_ref.at[pl.ds(w_ref.shape[0] - k, k)]
    put_blocks(t_ref, ga_ref, s_ref, w_others, lambda m: m * (span - HALO), True)
    put_sides(t_ref, ga_ref, z_ref, w_others, True)

    first_row = place_ref[0] * rows - HALO
    left = jnp.where(place_ref[1] > 0, 1.0, 0.0)
    right = jnp.where(place_ref[1] < limits[1] - 1, 1.0, 0.0)
    for step in range(SWEEPS):
        j = SWEEPS - 1 - step
        now, nxt = ((ga_ref, gb_ref), (gb_ref, ga_ref))[step % 2]
        reach = j + 2

        def sweep(x, _, now=now, nxt=nxt, j=j):
            row = first_row + x
            inside = jnp.where((row >= 0) & (row < limits[0] * rows), 1.0, 0.0)
            for y in range(8, wide - 8, 8):
                here = pl.ds(y, 8)
                total = (now[x - 1, here] + now[x + 1, here]) + (now[x, pl.ds(y - 1, 8)] + now[x, pl.ds(y + 1, 8)])
                mask = inside
                if y == 8:
                    mask = inside * left
                elif y == wide - 16:
                    mask = inside * right
                nxt[x, here] = (total + t_ref[j, x, pl.ds(y - 8, 8)]) * mask
            return _

        lax.fori_loop(HALO - reach, HALO + rows + reach, sweep, 0, unroll=4)

    done = (gb_ref, ga_ref)[(SWEEPS - 1) % 2]
    levels = u_rows.shape[1]

    def turn(x, _):
        h_rows[x] = done[x + HALO - 2, pl.ds(16, LANES)].T[:levels]
        return _

    lax.fori_loop(0, rows + 4, turn, 0, unroll=2)
    for copy in loads:
        copy.wait()

    def stores(x):
        return [
            pltpu.make_async_copy(src, dst.at[:, x, :], sems.at[i, x])
            for i, (src, dst) in enumerate(
                ((u_rows.at[x], east_ref), (v_rows.at[x], north_ref), (h_rows.at[x + 2], height_ref))
            )
        ]

    def output(x, _):
        def north(i):
            return done[x + HALO, pl.ds(16 + i, LANES)]

        dy = (8.0 * (north(1) - north(-1)) - (north(2) - north(-2))).T[:levels]
        dx = 8.0 * (h_rows[x + 3] - h_rows[x + 1]) - (h_rows[x + 4] - h_rows[x])
        u_rows[x] = u_rows[x] - dx * (1.0 / 12.0)
        v_rows[x] = v_rows[x] - dy * (1.0 / 12.0)
        for copy in stores(x):
            copy.start()
        return _

    lax.fori_loop(0, rows, output, 0, unroll=2)
    for x in range(rows):
        for copy in stores(x):
            copy.wait()

def shape(*dims, dtype=F32):
    return jax.ShapeDtypeStruct(dims, dtype)

def neighbours(axis):
    peers = lax.axis_size(axis)
    up = [(i, i + 1) for i in range(peers - 1)]
    return up, [(j, i) for i, j in up]

def on_device(east_wind, north_wind, height, to_modes, to_levels, mode_coef):
    levels, rows, cols = east_wind.shape
    groups = lax.axis_size("lev")
    limits = (lax.axis_size("gx"), lax.axis_size("gy"))
    lp, kp = up_to(levels, 8), up_to(levels, 16)
    span = rows + 2 * HALO
    x_up, x_down = neighbours("gx")
    y_up, y_down = neighbours("gy")
    dma = pltpu.SemaphoreType.DMA
    row_block = pltpu.VMEM((rows, levels, cols), F32)

    east_wind, north_wind, height = (
        pltpu.with_memory_space_constraint(value, pltpu.HBM) for value in (east_wind, north_wind, height)
    )

    def to_others(value):
        return [value] + [
            lax.ppermute(value, "lev", [((i + d) % groups, i) for i in range(groups)]) for d in range(1, groups)
        ]

    lo, hi, packed, mid = call(
        inner_rows,
        (
            shape(2, levels, LANES),
            shape(2, levels, LANES),
            shape(levels, LANES),
            shape(rows - 2 * HALO, lp, LANES),
        ),
        east_wind,
        north_wind,
        height,
        specs=[HBM] * 3,
        scratch=(row_block, row_block, row_block, dma((3, rows)), dma((4,))),
        name="inner_rows",
    )
    mids = to_others(mid)
    halo = (
        lax.ppermute(hi, "gx", x_up),
        lax.ppermute(lo, "gx", x_down),
        lax.ppermute(packed, "gy", y_up),
        lax.ppermute(packed, "gy", y_down),
    )

    me = lax.axis_index("lev")
    my_levels = lax.dynamic_slice_in_dim(to_levels, me * levels, levels, 0)
    my_levels = jnp.pad(my_levels, ((0, LANES - levels), (0, 0)))
    modes = []
    for d in range(groups):
        part = lax.dynamic_slice_in_dim(to_modes, (me + d) % groups * levels, levels, 1)
        modes.append(jnp.pad(part, ((0, 0), (0, kp - levels))))
    w = call(
        weights,
        shape(groups * 3 * kp, TERMS * LANES, dtype=BF16),
        my_levels,
        jnp.stack(modes),
        mode_coef.reshape(1, -1),
        name="weights",
    )
    place = jnp.stack([lax.axis_index("gx"), lax.axis_index("gy")]).astype(jnp.int32)
    low, high, pack = call(
        outer_rows,
        (shape(HALO, lp, LANES), shape(HALO, lp, LANES), shape(rows // 8 - 2, lp, LANES)),
        east_wind,
        north_wind,
        height,
        mid,
        specs=[HBM] * 3 + [VMEM],
        scratch=(row_block, row_block, row_block, dma((3, rows))),
        name="outer_rows",
    )
    halo, place, mids, low, high, pack = lax.optimization_barrier((halo, place, mids, low, high, pack))

    mids_rows = rows // 8 - 2
    low, high, pack, edge = call(
        outer_fix,
        (
            shape(HALO, lp, LANES),
            shape(HALO, lp, LANES),
            shape(mids_rows, lp, LANES),
            shape(2 * HALO + mids_rows, lp, LANES),
        ),
        low,
        high,
        pack,
        packed,
        *halo,
        name="outer_fix",
    )
    edges = to_others(edge)
    below = lax.ppermute(high, "gx", x_up)
    above = lax.ppermute(low, "gx", x_down)
    right, left = call(
        column_messages,
        (shape(span // 16, lp, LANES), shape(span // 16, lp, LANES)),
        low,
        high,
        pack,
        below,
        above,
        name="column_messages",
    )
    from_left = lax.ppermute(right, "gy", y_up)
    from_right = lax.ppermute(left, "gy", y_down)
    k = 3 * kp
    terms = (shape(SWEEPS, span, cols + 16, LANES), shape(span, cols + 32, LANES))
    t, g = call(
        mix_outer,
        terms,
        w,
        low,
        high,
        below,
        above,
        scratch=(pltpu.VMEM((4, k, 8 * LANES), BF16),),
        name="mix_outer",
    )
    edges, zl, zr, t, g = lax.optimization_barrier((edges, from_left, from_right, t, g))
    belows = [lax.ppermute(e[HALO : 2 * HALO], "gx", x_up) for e in edges[1:]]
    aboves = [lax.ppermute(e[:HALO], "gx", x_down) for e in edges[1:]]
    lefts, rights = to_others(zl), to_others(zr)

    operands = []
    for d in range(groups):
        operands += [edges[d], mids[d]]
    n = len(operands)
    t, g = call(
        functools.partial(mix_inner, groups=groups),
        terms,
        w,
        *operands,
        zl,
        zr,
        t,
        g,
        scratch=(
            pltpu.VMEM((rows // 8 - 2, groups * k, 8 * LANES), BF16),
            pltpu.VMEM((2, (groups - 1) * k, 8 * LANES), BF16),
            pltpu.VMEM((k, span // 8 * LANES), BF16),
        ),
        alias={n + 3: 0, n + 4: 1},
        name="mix_inner",
    )
    operands = []
    for d in range(groups - 1):
        operands += [belows[d], aboves[d], lefts[d + 1], rights[d + 1]]
    out = shape(levels, rows, cols)
    return call(
        functools.partial(finish, others=groups - 1, limits=limits),
        (shape(SWEEPS, span, cols + 16, LANES), shape(span, cols + 32, LANES), out, out, out),
        place,
        w,
        *operands,
        t,
        g,
        east_wind,
        north_wind,
        specs=[SMEM] + [VMEM] * (len(operands) + 3) + [HBM] * 2,
        out_specs=(VMEM, VMEM, HBM, HBM, HBM),
        scratch=(
            pltpu.VMEM((2, (groups - 1) * k, 8 * LANES), BF16),
            pltpu.VMEM(((groups - 1) * k, span // 8 * LANES), BF16),
            pltpu.VMEM((span, cols + 32, LANES), F32),
            row_block,
            row_block,
            pltpu.VMEM((rows + 4, levels, cols), F32),
            dma((3, rows)),
        ),
        alias={2 + len(operands): 0, 3 + len(operands): 1},
        name="finish",
    )[2:]


def solution(mesh):
    return jax.shard_map(
        on_device,
        mesh=mesh,
        in_specs=(P("lev", "gx", "gy"), P("lev", "gx", "gy"), P("lev", "gx", "gy"), P(), P(), P()),
        out_specs=(P("lev", "gx", "gy"), P("lev", "gx", "gy"), P("lev", "gx", "gy")),
        check_vma=False,
    )
```

```python
import functools

import jax
import jax.numpy as jnp
from jax import lax
from jax.experimental import pallas as pl
from jax.experimental.pallas import tpu as pltpu
from jax.sharding import PartitionSpec as P

SWEEPS = 6
HALO = SWEEPS + 2
TERMS = SWEEPS + 1
LANES = 128
VMEM = pl.BlockSpec(memory_space=pltpu.VMEM)
SMEM = pl.BlockSpec(memory_space=pltpu.SMEM)
HBM = pl.BlockSpec(memory_space=pltpu.HBM)
F32 = jnp.float32
BF16 = jnp.bfloat16

def up_to(n, k):
    return (n + k - 1) // k * k

def lanes_of():
    return lax.broadcasted_iota(jnp.int32, (1, LANES), 1)

def call(body, outs, *args, specs=None, out_specs=None, scratch=(), alias=None, vmem=12 << 20, name):
    return pl.pallas_call(
        body,
        out_shape=outs,
        in_specs=specs or [VMEM] * len(args),
        out_specs=out_specs or jax.tree.map(lambda _: VMEM, outs),
        scratch_shapes=list(scratch),
        input_output_aliases=alias or {},
        cost_estimate=pl.CostEstimate(flops=1, transcendentals=0, bytes_accessed=1),
        compiler_params=pltpu.CompilerParams(vmem_limit_bytes=vmem),
        name=name,
    )(*args)

def start_rows(src_ref, dst_ref, sems, rows):
    copies = {x: pltpu.make_async_copy(src_ref.at[:, x, :], dst_ref.at[x], sems.at[x]) for x in rows}
    for copy in copies.values():
        copy.start()
    return copies

def north_step(main, side):
    lane = lanes_of()
    one = pltpu.roll(jnp.where(lane < 1, side, main), LANES - 1, 1) - pltpu.roll(
        jnp.where(lane >= LANES - 1, side, main), 1, 1
    )
    two = pltpu.roll(jnp.where(lane < 2, side, main), LANES - 2, 1) - pltpu.roll(
        jnp.where(lane >= LANES - 2, side, main), 2, 1
    )
    return 8.0 * one - two

def source_row(x, at, v, h, side):
    dx = 8.0 * (at(x + 1) - at(x - 1)) - (at(x + 2) - at(x - 2))
    return h - (dx + north_step(v, side)) * (1.0 / 12.0)

def put_padded(ref, i, value):
    levels, pad = value.shape[0], ref.shape[1] - value.shape[0]
    ref[i, :levels] = value
    if pad:
        ref[i, levels:] = jnp.zeros((pad, LANES), F32)

def inner_rows(u_ref, v_ref, h_ref, lo_ref, hi_ref, cols_ref, mid_ref, u_rows, v_rows, h_rows, sems, edge_sems):
    rows = u_ref.shape[1]
    lane = lanes_of()
    edges = []
    for i in range(2):
        edges.append(pltpu.make_async_copy(u_ref.at[:, i, :], lo_ref.at[i], edge_sems.at[i]))
        edges.append(pltpu.make_async_copy(u_ref.at[:, rows - 2 + i, :], hi_ref.at[i], edge_sems.at[2 + i]))
    for copy in edges:
        copy.start()
    v_loads = start_rows(v_ref, v_rows, sems.at[0], range(rows))
    u_loads = start_rows(u_ref, u_rows, sems.at[1], range(HALO - 2, rows - HALO + 2))
    h_loads = start_rows(h_ref, h_rows, sems.at[2], range(HALO, rows - HALO))
    for copy in v_loads.values():
        copy.wait()
    packed = None
    for x in range(rows):
        rolled = pltpu.roll(v_rows[x], (4 * x + 2) % LANES, 1)
        packed = rolled if packed is None else jnp.where(lane // 4 == x, rolled, packed)
    cols_ref[...] = packed
    for copy in (*u_loads.values(), *h_loads.values()):
        copy.wait()
    for x in range(HALO, rows - HALO):
        put_padded(mid_ref, x - HALO, source_row(x, lambda i: u_rows[i], v_rows[x], h_rows[x], v_rows[x]))
    for copy in edges:
        copy.wait()

def outer_rows(u_ref, v_ref, h_ref, mid_ref, low_ref, high_ref, pack_ref, u_rows, v_rows, h_rows, sems):
    rows, levels, _ = u_rows.shape
    lane = lanes_of()
    ends = [*range(HALO), *range(rows - HALO, rows)]
    wide = [*range(HALO + 2), *range(rows - HALO - 2, rows)]
    loads = [
        *start_rows(v_ref, v_rows, sems.at[1], ends).values(),
        *start_rows(u_ref, u_rows, sems.at[0], wide).values(),
        *start_rows(h_ref, h_rows, sems.at[2], ends).values(),
    ]
    for m in range(pack_ref.shape[0]):
        packed = pltpu.roll(mid_ref[8 * m], 8, 1)
        for k in range(1, 8):
            packed = jnp.where(lane // 16 == k, pltpu.roll(mid_ref[8 * m + k], (16 * k + 8) % LANES, 1), packed)
        pack_ref[m] = packed
    for copy in loads:
        copy.wait()

    def at(x):
        return u_rows[x] if 0 <= x < rows else jnp.zeros((levels, LANES), F32)

    for x in ends:
        s = source_row(x, at, v_rows[x], h_rows[x], v_rows[x])
        if x < HALO:
            put_padded(low_ref, x, s)
        else:
            put_padded(high_ref, x - rows + HALO, s)

def column_terms(own_ref, left_ref, right_ref):
    slot = lanes_of() % 4
    d = jnp.where(slot < 2, left_ref[...], right_ref[...]) - own_ref[...]
    far = jnp.where(slot < 2, pltpu.roll(d, LANES - 2, 1), -pltpu.roll(d, 2, 1))
    near = jnp.where(slot == 1, -pltpu.roll(d, LANES - 1, 1), jnp.where(slot == 2, pltpu.roll(d, 1, 1), 0.0))
    return (far + 8.0 * near) * (1.0 / 12.0)

def outer_fix(low_in, high_in, pack_in, own_ref, ulo_ref, uhi_ref, vl_ref, vr_ref, low_ref, high_ref, pack_ref, edge_ref):
    levels = own_ref.shape[0]
    lane = lanes_of()
    rows = LANES // 4
    terms = column_terms(own_ref, vl_ref, vr_ref)
    edge = (lane < 2) | (lane >= LANES - 2)
    below = {0: 8.0 * ulo_ref[1] - ulo_ref[0], 1: -ulo_ref[1]}
    above = {HALO - 1: uhi_ref[1] - 8.0 * uhi_ref[0], HALO - 2: uhi_ref[0]}
    for ref_in, ref, x0, at, more in (
        (high_in, high_ref, rows - HALO, HALO, above),
        (low_in, low_ref, 0, 0, below),
    ):
        for i in range(HALO):
            add = jnp.where(edge, pltpu.roll(terms, (LANES - 4 * (x0 + i) - 2) % LANES, 1), 0.0)
            if i in more:
                add = add + more[i] * (1.0 / 12.0)
            value = ref_in[i, :levels] + add
            put_padded(ref, i, value)
            put_padded(edge_ref, at + i, value)
    slot = lane % 16
    for m in range(pack_ref.shape[0]):
        add = jnp.zeros((levels, LANES), F32)
        for k in range(8):
            x = HALO + 8 * m + k
            here = (lane // 16 == k) & (slot >= 6) & (slot < 10)
            add = jnp.where(here, pltpu.roll(terms, (16 * k + 6 - 4 * x) % LANES, 1), add)
        value = pack_in[m, :levels] + add
        put_padded(pack_ref, m, value)
        put_padded(edge_ref, 2 * HALO + m, value)


def column_messages(low_ref, high_ref, pack_ref, below_ref, above_ref, right_ref, left_ref):
    lane = lanes_of()
    slot = lane % 16

    def pack(ref):
        packed = pltpu.roll(ref[0], 8, 1)
        for k in range(1, 8):
            packed = jnp.where(lane // 16 == k, pltpu.roll(ref[k], (16 * k + 8) % LANES, 1), packed)
        return packed

    packs = [pack(below_ref), pack(low_ref)]
    packs += [pack_ref[i] for i in range(pack_ref.shape[0])]
    packs += [pack(high_ref), pack(above_ref)]
    for i in range(len(packs) // 2):
        even, odd = packs[2 * i], packs[2 * i + 1]
        right_ref[i] = jnp.where(slot < 8, even, pltpu.roll(odd, 8, 1))
        left_ref[i] = jnp.where(slot < 8, pltpu.roll(even, LANES - 8, 1), odd)

def weights(levels_ref, modes_ref, coef_ref, out_ref):
    groups, _, kp = modes_ref.shape
    coef = coef_ref[...]
    denom = 1.0 + 4.0 * coef
    scaled = levels_ref[...] / denom
    ratio = coef / denom
    for j in range(TERMS):
        at = pl.ds(j * LANES, LANES)
        for g in range(groups):
            m = jnp.dot(scaled, modes_ref[g], precision=lax.Precision.HIGHEST, preferred_element_type=F32).T
            high = m.astype(BF16)
            low = (m - high.astype(F32)).astype(BF16)
            for i, part in enumerate((high, high, low)):
                out_ref[pl.ds((3 * g + i) * kp, kp), at] = part
        scaled = scaled * ratio

def parts(value, kp):
    if kp > value.shape[0]:
        value = jnp.concatenate([value, jnp.zeros((kp - value.shape[0], LANES), F32)], axis=0)
    high = value.astype(BF16)
    low = (value - high.astype(F32)).astype(BF16)
    return high, low, high

def stage_block(s_ref, m, g, kp, ref, fix=None):
    lane = lanes_of()
    outer = (lane < HALO) | (lane >= LANES - HALO)

    def stage(k, _):
        value = ref[k]
        if fix is not None:
            value = jnp.where(outer, pltpu.roll(fix, LANES - 16 * k - 8, 1), value)
        at = pl.ds(pl.multiple_of(k * LANES, LANES), LANES)
        for i, part in enumerate(parts(value, kp)):
            s_ref[m, pl.ds((3 * g + i) * kp, kp), at] = part
        return _

    lax.fori_loop(0, 8, stage, 0, unroll=8)

def stage_sides(z_ref, g, kp, left_ref, right_ref):
    slot = lanes_of() % 16
    for m in range(z_ref.shape[1] // LANES):
        zl, zr = left_ref[m // 2], right_ref[m // 2]
        if m % 2 == 0:
            side = jnp.where(slot < 8, zl, pltpu.roll(zr, 8, 1))
        else:
            side = jnp.where(slot < 8, pltpu.roll(zl, LANES - 8, 1), zr)
        for i, part in enumerate(parts(side, kp)):
            z_ref[pl.ds((3 * g + i) * kp, kp), m * LANES : (m + 1) * LANES] = part

def mix(operand, w_ref):
    return lax.dot_general(operand, w_ref[...], (((0,), (0,)), ((), ())), preferred_element_type=F32)

def put(t_ref, g_ref, x, col, part, add):
    at = pl.ds(col, part.shape[0])
    for j in range(TERMS):
        value = part[:, j * LANES : (j + 1) * LANES]
        if j == SWEEPS:
            at = pl.ds(col + 8, part.shape[0])
            g_ref[x, at] = g_ref[x, at] + value if add else value
        else:
            t_ref[j, x, at] = t_ref[j, x, at] + value if add else value

def put_blocks(t_ref, g_ref, s_ref, w_ref, row_of_block, add):
    def block(m, _):
        part = mix(s_ref[m], w_ref)
        for k in range(8):
            put(t_ref, g_ref, row_of_block(m) + k, HALO, part[k * LANES : (k + 1) * LANES], add)
        return _

    lax.fori_loop(0, s_ref.shape[0], block, 0, unroll=2)

def put_sides(t_ref, g_ref, z_ref, w_ref, add):
    part = mix(z_ref[...], w_ref)
    for x in range(g_ref.shape[0]):
        put(t_ref, g_ref, x, 0, part[16 * x : 16 * x + 8], add)
        put(t_ref, g_ref, x, HALO + LANES, part[16 * x + 8 : 16 * x + 16], add)


def mix_outer(w_ref, low, high, below, above, t_ref, g_ref, s_ref):
    span, wide, _ = g_ref.shape
    kp = s_ref.shape[1] // 3
    g_ref[:, :8] = jnp.zeros((span, 8, LANES), F32)
    g_ref[:, wide - 8 :] = jnp.zeros((span, 8, LANES), F32)
    for m, ref in enumerate((below, low, high, above)):
        stage_block(s_ref, m, 0, kp, ref)
    far = span - 4 * HALO
    put_blocks(t_ref, g_ref, s_ref, w_ref.at[pl.ds(0, 3 * kp)], lambda m: HALO * m + jnp.where(m > 1, far, 0), False)


def mix_inner(w_ref, *refs, groups):
    ins, (zl, zr, _, _, t_ref, g_ref, s_ref, r_ref, z_ref) = refs[: 2 * groups], refs[2 * groups :]
    span, wide, _ = g_ref.shape
    k = z_ref.shape[0]
    kp = k // 3
    w_own = w_ref.at[pl.ds(0, k)]
    w_others = w_ref.at[pl.ds(k, k * (groups - 1))]
    stage_sides(z_ref, 0, kp, zl, zr)
    put_sides(t_ref, g_ref, z_ref, w_own, False)
    for g in range(groups):
        edge, mid = ins[2 * g : 2 * g + 2]
        for i in range(mid.shape[0] // 8):
            stage_block(s_ref, i, g, kp, mid.at[pl.ds(8 * i, 8)], edge[2 * HALO + i])
        if g > 0:
            stage_block(r_ref, 0, g - 1, kp, edge.at[pl.ds(0, HALO)])
            stage_block(r_ref, 1, g - 1, kp, edge.at[pl.ds(HALO, HALO)])
    put_blocks(t_ref, g_ref, r_ref, w_others, lambda m: HALO + (span - 3 * HALO) * m, True)
    put_blocks(t_ref, g_ref, s_ref, w_ref, lambda m: 2 * HALO + 8 * m, False)


def finish(place_ref, w_ref, *refs, others, limits):
    ins, refs = refs[: 4 * others], refs[4 * others :]
    _, _, u_ref, v_ref, t_ref, ga_ref, east_ref, north_ref, height_ref, s_ref, z_ref, gb_ref, u_rows, v_rows, h_rows, sems = refs
    span, wide, _ = ga_ref.shape
    rows = span - 2 * HALO
    loads = [*start_rows(u_ref, u_rows, sems.at[0], range(rows)).values()]
    loads += start_rows(v_ref, v_rows, sems.at[1], range(rows)).values()
    gb_ref[:, :8] = jnp.zeros((span, 8, LANES), F32)
    gb_ref[:, wide - 8 :] = jnp.zeros((span, 8, LANES), F32)
    k = s_ref.shape[1]
    for d in range(others):
        below, above, zl, zr = ins[4 * d : 4 * d + 4]
        kp = k // (3 * others)
        stage_block(s_ref, 0, d, kp, below)
        stage_block(s_ref, 1, d, kp, above)
        stage_sides(z_ref, d, kp, zl, zr)
    w_others = w_ref.at[pl.ds(w_ref.shape[0] - k, k)]
    put_blocks(t_ref, ga_ref, s_ref, w_others, lambda m: m * (span - HALO), True)
    put_sides(t_ref, ga_ref, z_ref, w_others, True)

    first_row = place_ref[0] * rows - HALO
    left = jnp.where(place_ref[1] > 0, 1.0, 0.0)
    right = jnp.where(place_ref[1] < limits[1] - 1, 1.0, 0.0)
    for step in range(SWEEPS):
        j = SWEEPS - 1 - step
        now, nxt = ((ga_ref, gb_ref), (gb_ref, ga_ref))[step % 2]
        reach = j + 2

        def sweep(x, _, now=now, nxt=nxt, j=j):
            row = first_row + x
            inside = jnp.where((row >= 0) & (row < limits[0] * rows), 1.0, 0.0)
            for y in range(8, wide - 8, 8):
                here = pl.ds(y, 8)
                total = (now[x - 1, here] + now[x + 1, here]) + (now[x, pl.ds(y - 1, 8)] + now[x, pl.ds(y + 1, 8)])
                mask = inside
                if y == 8:
                    mask = inside * left
                elif y == wide - 16:
                    mask = inside * right
                nxt[x, here] = (total + t_ref[j, x, pl.ds(y - 8, 8)]) * mask
            return _

        lax.fori_loop(HALO - reach, HALO + rows + reach, sweep, 0, unroll=8)

    done = (gb_ref, ga_ref)[(SWEEPS - 1) % 2]
    levels = u_rows.shape[1]

    def turn(x, _):
        h_rows[x] = done[x + HALO - 2, pl.ds(16, LANES)].T[:levels]
        return _

    lax.fori_loop(0, rows + 4, turn, 0, unroll=12)
    for copy in loads:
        copy.wait()

    def stores(x):
        return [
            pltpu.make_async_copy(src, dst.at[:, x, :], sems.at[i, x])
            for i, (src, dst) in enumerate(
                ((u_rows.at[x], east_ref), (v_rows.at[x], north_ref), (h_rows.at[x + 2], height_ref))
            )
        ]

    def output(x, _):
        def north(i):
            return done[x + HALO, pl.ds(16 + i, LANES)]

        dy = (8.0 * (north(1) - north(-1)) - (north(2) - north(-2))).T[:levels]
        dx = 8.0 * (h_rows[x + 3] - h_rows[x + 1]) - (h_rows[x + 4] - h_rows[x])
        u_rows[x] = u_rows[x] - dx * (1.0 / 12.0)
        v_rows[x] = v_rows[x] - dy * (1.0 / 12.0)
        for copy in stores(x):
            copy.start()
        return _

    lax.fori_loop(0, rows, output, 0, unroll=8)
    for x in range(rows):
        for copy in stores(x):
            copy.wait()

def shape(*dims, dtype=F32):
    return jax.ShapeDtypeStruct(dims, dtype)

def neighbours(axis):
    peers = lax.axis_size(axis)
    up = [(i, i + 1) for i in range(peers - 1)]
    return up, [(j, i) for i, j in up]

def on_device(east_wind, north_wind, height, to_modes, to_levels, mode_coef):
    levels, rows, cols = east_wind.shape
    groups = lax.axis_size("lev")
    limits = (lax.axis_size("gx"), lax.axis_size("gy"))
    lp, kp = up_to(levels, 8), up_to(levels, 16)
    span = rows + 2 * HALO
    x_up, x_down = neighbours("gx")
    y_up, y_down = neighbours("gy")
    dma = pltpu.SemaphoreType.DMA
    row_block = pltpu.VMEM((rows, levels, cols), F32)

    east_wind, north_wind, height = (
        pltpu.with_memory_space_constraint(value, pltpu.HBM) for value in (east_wind, north_wind, height)
    )

    def to_others(value):
        return [value] + [
            lax.ppermute(value, "lev", [((i + d) % groups, i) for i in range(groups)]) for d in range(1, groups)
        ]

    lo, hi, packed, mid = call(
        inner_rows,
        (
            shape(2, levels, LANES),
            shape(2, levels, LANES),
            shape(levels, LANES),
            shape(rows - 2 * HALO, lp, LANES),
        ),
        east_wind,
        north_wind,
        height,
        specs=[HBM] * 3,
        scratch=(row_block, row_block, row_block, dma((3, rows)), dma((4,))),
        name="inner_rows",
    )
    mids = to_others(mid)
    halo = (
        lax.ppermute(hi, "gx", x_up),
        lax.ppermute(lo, "gx", x_down),
        lax.ppermute(packed, "gy", y_up),
        lax.ppermute(packed, "gy", y_down),
    )

    me = lax.axis_index("lev")
    my_levels = lax.dynamic_slice_in_dim(to_levels, me * levels, levels, 0)
    my_levels = jnp.pad(my_levels, ((0, LANES - levels), (0, 0)))
    modes = []
    for d in range(groups):
        part = lax.dynamic_slice_in_dim(to_modes, (me + d) % groups * levels, levels, 1)
        modes.append(jnp.pad(part, ((0, 0), (0, kp - levels))))
    w = call(
        weights,
        shape(groups * 3 * kp, TERMS * LANES, dtype=BF16),
        my_levels,
        jnp.stack(modes),
        mode_coef.reshape(1, -1),
        name="weights",
    )
    place = jnp.stack([lax.axis_index("gx"), lax.axis_index("gy")]).astype(jnp.int32)
    low, high, pack = call(
        outer_rows,
        (shape(HALO, lp, LANES), shape(HALO, lp, LANES), shape(rows // 8 - 2, lp, LANES)),
        east_wind,
        north_wind,
        height,
        mid,
        specs=[HBM] * 3 + [VMEM],
        scratch=(row_block, row_block, row_block, dma((3, rows))),
        name="outer_rows",
    )
    halo, place, mids, low, high, pack = lax.optimization_barrier((halo, place, mids, low, high, pack))

    mids_rows = rows // 8 - 2
    low, high, pack, edge = call(
        outer_fix,
        (
            shape(HALO, lp, LANES),
            shape(HALO, lp, LANES),
            shape(mids_rows, lp, LANES),
            shape(2 * HALO + mids_rows, lp, LANES),
        ),
        low,
        high,
        pack,
        packed,
        *halo,
        name="outer_fix",
    )
    edges = to_others(edge)
    below = lax.ppermute(high, "gx", x_up)
    above = lax.ppermute(low, "gx", x_down)
    right, left = call(
        column_messages,
        (shape(span // 16, lp, LANES), shape(span // 16, lp, LANES)),
        low,
        high,
        pack,
        below,
        above,
        name="column_messages",
    )
    from_left = lax.ppermute(right, "gy", y_up)
    from_right = lax.ppermute(left, "gy", y_down)
    k = 3 * kp
    terms = (shape(SWEEPS, span, cols + 16, LANES), shape(span, cols + 32, LANES))
    t, g = call(
        mix_outer,
        terms,
        w,
        low,
        high,
        below,
        above,
        scratch=(pltpu.VMEM((4, k, 8 * LANES), BF16),),
        name="mix_outer",
    )
    edges, zl, zr, t, g = lax.optimization_barrier((edges, from_left, from_right, t, g))
    belows = [lax.ppermute(e[HALO : 2 * HALO], "gx", x_up) for e in edges[1:]]
    aboves = [lax.ppermute(e[:HALO], "gx", x_down) for e in edges[1:]]
    lefts, rights = to_others(zl), to_others(zr)

    operands = []
    for d in range(groups):
        operands += [edges[d], mids[d]]
    n = len(operands)
    t, g = call(
        functools.partial(mix_inner, groups=groups),
        terms,
        w,
        *operands,
        zl,
        zr,
        t,
        g,
        scratch=(
            pltpu.VMEM((rows // 8 - 2, groups * k, 8 * LANES), BF16),
            pltpu.VMEM((2, (groups - 1) * k, 8 * LANES), BF16),
            pltpu.VMEM((k, span // 8 * LANES), BF16),
        ),
        alias={n + 3: 0, n + 4: 1},
        name="mix_inner",
    )
    operands = []
    for d in range(groups - 1):
        operands += [belows[d], aboves[d], lefts[d + 1], rights[d + 1]]
    out = shape(levels, rows, cols)
    return call(
        functools.partial(finish, others=groups - 1, limits=limits),
        (shape(SWEEPS, span, cols + 16, LANES), shape(span, cols + 32, LANES), out, out, out),
        place,
        w,
        *operands,
        t,
        g,
        east_wind,
        north_wind,
        specs=[SMEM] + [VMEM] * (len(operands) + 3) + [HBM] * 2,
        out_specs=(VMEM, VMEM, HBM, HBM, HBM),
        scratch=(
            pltpu.VMEM((2, (groups - 1) * k, 8 * LANES), BF16),
            pltpu.VMEM(((groups - 1) * k, span // 8 * LANES), BF16),
            pltpu.VMEM((span, cols + 32, LANES), F32),
            row_block,
            row_block,
            pltpu.VMEM((rows + 4, levels, cols), F32),
            dma((3, rows)),
        ),
        alias={2 + len(operands): 0, 3 + len(operands): 1},
        name="finish",
    )[2:]


def solution(mesh):
    return jax.shard_map(
        on_device,
        mesh=mesh,
        in_specs=(P("lev", "gx", "gy"), P("lev", "gx", "gy"), P("lev", "gx", "gy"), P(), P(), P()),
        out_specs=(P("lev", "gx", "gy"), P("lev", "gx", "gy"), P("lev", "gx", "gy")),
        check_vma=False,
    )
```
